128 devices in a mesh: row: 8 (over z_hi, x), col: 16 (over y, z_lo, core).
Axes of the slice: x: 4, y: 4, z: 4 (z_hi: 2, z_lo: 2; z = z_hi * 2 + z_lo), core: 2. Of those that a mesh axis runs over, the one named last changes fastest.
Arguments:
- traces: bfloat16 [64, 16384], P(None, ('row', 'col')), may hold values from -6 to 6
- incident: bfloat16 [64, 16384], P(None, ('row', 'col')), may hold values from -6 to 6
- points: float32 [3, 16384], P(None, ('row', 'col')), may hold values from 0 to 1
- coupling: int32 [16384], P(('row', 'col')), may hold values from 0 to 2047, as said below
- volume_tiles: bfloat16 [32, 64, 4, 128, 128], P('row', 'col'), may hold values from -0.125 to 0.125
- tile_columns: int32 [32, 64, 4], P('row', 'col'), may hold values from 0 to 8, as said below
Outputs:
- traces_out: bfloat16 [64, 16384], P(None, ('row', 'col'))
- volume_out: float32 [64, 32, 64, 128], P(None, 'row', 'col')
The draws below stay inside these ranges and needn't reach their ends.
Inputs may be any that keep to these rules, and one draw needn't show every extreme that they name: `coupling`: within each aligned block of 128 unknowns the values are distinct. `tile_columns`: the 4 entries of one tile are distinct, and one of them is 4.
All inputs are finite; a program needn't handle non-finite values.
Results may differ from the reference program's by a relative error of at most 0.0154.
Values may be sent and summed in bfloat16 or wider, within the bound.
No kernel may reach another device: no remote copies, remote signals or barrier semaphores. Data moves between devices by JAX's collectives and lax.ppermute only.
A program may use at most 64 MiB of HBM per device.

```python
import math
import jax
import jax.numpy as jnp
from jax import lax

EXCITE = 64
SURF_DEV = 128
TILES_Y = 4
TILES_X = 4
TILE_SIDE = 128
TILE_COUNT = 4
OUTER_STEPS = 2
PASSES = 2
SURFACE = 16384
GRID_Y = 32
GRID_X = 64
N_ROW = 8
N_COL = 16


def draw_coupling(key, part):
    vol_rows = TILES_Y * TILES_X * TILE_SIDE
    block_count = SURFACE // SURF_DEV
    keys = jax.random.split(jax.random.fold_in(key, 7), block_count)

    def one_block(subkey):
        return jax.random.permutation(subkey, vol_rows)[:SURF_DEV]
    values = jax.vmap(one_block)(keys).astype(jnp.int32)
    inner = (jax.random.permutation(jax.random.fold_in(key, 8), vol_rows - 2)[:SURF_DEV - 2] + 1).astype(jnp.int32)
    ends = jnp.array([0, vol_rows - 1], jnp.int32)
    first_block = jax.random.permutation(jax.random.fold_in(key, 9), jnp.concatenate([ends, inner]))
    values = values.at[0].set(first_block)
    return values.reshape(SURFACE).astype(jnp.int32)


def draw_tile_columns(key, part):
    count_all = GRID_Y * GRID_X
    others = jnp.array([0, 1, 2, 3, 5, 6, 7, 8], jnp.int32)
    keys_pick = jax.random.split(jax.random.fold_in(key, 11), count_all)
    keys_order = jax.random.split(jax.random.fold_in(key, 12), count_all)

    def pick_others(subkey):
        return jax.random.permutation(subkey, others)[:TILE_COUNT - 1]
    picks = jax.vmap(pick_others)(keys_pick)
    centre = jnp.full((count_all, 1), 4, jnp.int32)
    full = jnp.concatenate([picks, centre], axis=1)

    def order_one(subkey):
        return jax.random.permutation(subkey, TILE_COUNT)
    order = jax.vmap(order_one)(keys_order)
    mixed = jnp.take_along_axis(full, order, axis=1)
    return mixed.reshape(GRID_Y, GRID_X, TILE_COUNT).astype(jnp.int32)


def shard_levels(own_key, dims, cuts, least, high):
    gain, own = 1.0, jax.random.fold_in(own_key, 6)
    for dim, parts in cuts:
        draws = jnp.exp(jax.random.uniform(jax.random.fold_in(own, dim), (parts,), jnp.float32, least / len(cuts), high / len(cuts)))
        gain = gain * jnp.repeat(draws, dims[dim] // parts).reshape([-1 if axis == dim else 1 for axis in range(len(dims))])
    return gain


def centred(rng, dims, scale, bound, shards=(), kind=jnp.bfloat16):
    drawn = jax.random.normal(rng, dims, jnp.float32) * scale
    if len(shards) > 0:
        drawn = shard_levels(rng, dims, shards, -0.22, 0.18) * drawn
    return jnp.clip(drawn, min=-bound, max=bound).astype(kind)


def setup_inputs(seed: int = 0) -> dict:
    splits = jax.random.split(jax.random.key(seed), 7)
    return {
        "traces": centred(splits[0], (EXCITE, SURFACE), 1.0, 6.0, ((1, 128),)),
        "incident": centred(splits[1], (EXCITE, SURFACE), 1.0, 6.0, ((1, 128),)),
        "points": jnp.clip(1.0 * jax.random.uniform(splits[2], (3, SURFACE), jnp.float32) ** shard_levels(splits[2], (3, SURFACE), ((1, 128),), -0.2, 0.2), 0.0, 1.0),
        "coupling": draw_coupling(jax.random.fold_in(splits[6], 71), 0),
        "volume_tiles": centred(splits[4], (GRID_Y, GRID_X, TILE_COUNT, TILE_SIDE, TILE_SIDE), (4 * TILE_COUNT * TILE_SIDE) ** -0.5, 0.125, ((0, 8), (1, 16))),
        "tile_columns": draw_tile_columns(jax.random.fold_in(splits[6], 71), 0),
    }


def wave_constants(total):
    spacing = float(total) ** (-1.0 / 3.0)
    return (2.0 / spacing, (0.5 * spacing) ** 2, 1.0 / math.sqrt(2.0 * total))

def kernel_block(source_points, target_points, consts):
    wave, smooth, factor = consts
    delta_x = source_points[0][:, None] - target_points[0][None, :]
    delta_y = source_points[1][:, None] - target_points[1][None, :]
    delta_z = source_points[2][:, None] - target_points[2][None, :]
    radius = jnp.sqrt(delta_x * delta_x + delta_y * delta_y + delta_z * delta_z + smooth)
    return (factor * jnp.cos(wave * radius) / radius).astype(jnp.bfloat16)

def apply_tiles(rounded, volume_tiles, tile_columns):
    padded = jnp.pad(rounded, ((0, 0), (1, 1), (1, 1), (0, 0)))
    picked = jnp.zeros(rounded.shape[:3] + (TILE_COUNT, TILE_SIDE), jnp.bfloat16)
    for offset in range(9):
        first = offset // 3
        second = offset % 3
        view = padded[:, first:first + GRID_Y, second:second + GRID_X, :]
        picked = jnp.where((tile_columns == offset)[None, :, :, :, None], view[:, :, :, None, :], picked)
    return jnp.einsum('eyxkq,yxkpq->eyxp', picked.astype(jnp.float32), volume_tiles.astype(jnp.float32))

def to_grid(local_rows):
    shaped = local_rows.reshape(EXCITE, N_ROW, N_COL, TILES_Y, TILES_X, TILE_SIDE)
    return shaped.transpose(0, 1, 3, 2, 4, 5).reshape(EXCITE, GRID_Y, GRID_X, TILE_SIDE)

def from_grid(field):
    shaped = field.reshape(EXCITE, N_ROW, TILES_Y, N_COL, TILES_X, TILE_SIDE)
    return shaped.transpose(0, 1, 3, 2, 4, 5).reshape(EXCITE, N_ROW, N_COL, TILES_Y * TILES_X * TILE_SIDE)

def reference(traces, incident, points, coupling, volume_tiles, tile_columns):
    consts = wave_constants(SURFACE)
    block_len = min(256, SURFACE)
    block_count = SURFACE // block_len
    target_blocks = points.reshape(3, block_count, block_len).transpose(1, 0, 2)
    row_index = jnp.arange(N_ROW, dtype=jnp.int32)[:, None, None]
    col_index = jnp.arange(N_COL, dtype=jnp.int32)[None, :, None]
    couple_grid = coupling.reshape(N_ROW, N_COL, SURF_DEV).astype(jnp.int32)
    vol_rows = TILES_Y * TILES_X * TILE_SIDE
    present = traces
    field = jnp.zeros((EXCITE, GRID_Y, GRID_X, TILE_SIDE), jnp.float32)
    for outer in range(OUTER_STEPS):

        def one_block(targets, present=present):
            kernel = kernel_block(points, targets, consts)
            return jnp.dot(present, kernel, preferred_element_type=jnp.float32)
        currents = lax.map(one_block, target_blocks)
        currents = currents.transpose(1, 0, 2).reshape(EXCITE, N_ROW, N_COL, SURF_DEV)
        local_source = jnp.zeros((EXCITE, N_ROW, N_COL, vol_rows), jnp.float32)
        local_source = local_source.at[:, row_index, col_index, couple_grid].set(currents)
        source = to_grid(local_source)
        field = source
        for sweep in range(PASSES):
            rounded = field.astype(jnp.bfloat16)
            field = source + apply_tiles(rounded, volume_tiles, tile_columns)
        readout = from_grid(field)[:, row_index, col_index, couple_grid].reshape(EXCITE, SURFACE)
        present = (incident.astype(jnp.float32) + readout).astype(jnp.bfloat16)
    return (present, field)
```

```python
import math

import jax
import jax.numpy as jnp
from jax import lax
from jax.experimental import pallas as pl
from jax.experimental.pallas import tpu as pltpu
from jax.sharding import PartitionSpec as P

E, U, S = 64, 128, 128
NR, NC = 8, 16
TOTAL = U * NR * NC
MB = 1 << 20
BF, F32 = jnp.bfloat16, jnp.float32
COS = (0.99999922, -19.73898252, 64.92872661, -85.27239691, 58.79403824, -21.07678136)
NT = (((1,), (1,)), ((), ()))
TN = (((0,), (0,)), ((), ()))

SPACING = float(TOTAL) ** (-1.0 / 3.0)
TURNS = 2.0 / SPACING / (2.0 * math.pi)
SMOOTH = (0.5 * SPACING) ** 2 * TURNS * TURNS
FACTOR = TURNS / math.sqrt(2.0 * TOTAL)


def dot(a, b, dims=(((1,), (0,)), ((), ()))):
    return lax.dot_general(a, b, dims, preferred_element_type=F32)


def call(body, out_shape, *, limit=24 * MB, flops=0, moved=0, **kwargs):
    return pl.pallas_call(
        body,
        out_shape=out_shape,
        compiler_params=pltpu.CompilerParams(vmem_limit_bytes=limit),
        cost_estimate=pl.CostEstimate(flops=flops, bytes_accessed=moved, transcendentals=0),
        **kwargs,
    )


def shape(dims, dtype):
    return jax.ShapeDtypeStruct(dims, dtype)


def split3(x):
    a = x.astype(BF).astype(F32)
    b = (x - a).astype(BF).astype(F32)
    return a, b, (x - a - b).astype(BF).astype(F32)


def rows_at(line, pieces):
    out = jnp.zeros((16, U), F32)
    for at, value in pieces:
        out = jnp.where(line == at, value, out)
    return out


def pack_body(traces, points, row_out, col_out):
    p = (points[...] - 0.5) * TURNS
    parts = split3(p)
    norm = jnp.sum(p * p, axis=0, keepdims=True)
    line = lax.broadcasted_iota(jnp.int32, (16, U), 0)
    source = [(3 * i + d, parts[i][d : d + 1]) for i in range(3) for d in range(3)]
    source += [(9 + i, v) for i, v in enumerate(split3(norm))] + [(12, 1.0)]
    source = rows_at(line, source).astype(BF)
    shifted = split3(norm + SMOOTH)
    target = []
    for j in range(3):
        pieces = [(3 * i + d, -2.0 * parts[j][d : d + 1]) for i in range(3) for d in range(3)]
        if j == 0:
            pieces += [(9 + i, 1.0) for i in range(3)]
        target.append(rows_at(line, pieces + [(12, shifted[j])]).astype(BF))
    for r in range(NR):
        for j in range(3):
            row_out[r, 16 * j : 16 * j + 16] = target[j]
    for c in range(NC):
        col_out[c, :E] = traces[...]
        col_out[c, E:] = source


def pack(traces, points):
    return call(pack_body, (shape((NR, 48, U), BF), shape((NC, E + 16, U), BF)))(traces, points)


def write_partials(acc, out):
    for d in range(NR):
        for j in range(3):
            b = d - 1 + j
            if 0 <= b < NR:
                out[d, j] = acc[:, b * U : b * U + U].astype(BF)
            else:
                out[d, j] = jnp.zeros((E, U), BF)


def kernel_body(col_ref, row_ref, k_ref, out_ref, acc, feats, dist):
    step = pl.program_id(0)

    @pl.when(step == 0)
    def _():
        for r in range(NR):
            feats[:, r * U : r * U + U] = row_ref[r]
        acc[...] = jnp.zeros_like(acc)

    for i in range(2):
        own = col_ref[i, E:]
        dist[i * U : i * U + U] = dot(jnp.concatenate([own, own, own], axis=0), feats[...], TN)

    def chunk(n, carry):
        at = pl.multiple_of(n * 16, 16)
        for h in range(2):
            d2 = dist[pl.ds(at, 16), h * 512 : h * 512 + 512]
            inv = lax.rsqrt(d2)
            turns = d2 * inv
            f = turns - jnp.round(turns)
            u = f * f
            value = COS[5] * FACTOR * u + COS[4] * FACTOR
            for c in COS[3::-1]:
                value = value * u + c * FACTOR
            k_ref[pl.ds(at, 16), h * 512 : h * 512 + 512] = (value * inv).astype(BF)
        return carry

    lax.fori_loop(0, 16, chunk, 0, unroll=2)
    p = jnp.concatenate([col_ref[0, :E], col_ref[1, :E]], axis=1)
    acc[...] += dot(p, k_ref[...])

    @pl.when(step == pl.num_programs(0) - 1)
    def _():
        write_partials(acc, out_ref)


def make_kernel(cols, rows):
    return call(
        kernel_body,
        (shape((NC * U, NR * U), BF), shape((NR, 3, E, U), BF)),
        flops=40 * 2 * MB,
        moved=6 * MB,
        grid=(NC // 2,),
        in_specs=[
            pl.BlockSpec((2, E + 16, U), lambda i: (i, 0, 0)),
            pl.BlockSpec((NR, 48, U), lambda i: (0, 0, 0)),
        ],
        out_specs=(
            pl.BlockSpec((2 * U, NR * U), lambda i: (i, 0)),
            pl.BlockSpec((NR, 3, E, U), lambda i: (0, 0, 0, 0)),
        ),
        scratch_shapes=[
            pltpu.VMEM((E, NR * U), F32),
            pltpu.VMEM((48, NR * U), BF),
            pltpu.VMEM((2 * U, NR * U), F32),
        ],
    )(cols, rows)


def product_body(p_ref, k_ref, out_ref, acc):
    step = pl.program_id(0)

    @pl.when(step == 0)
    def _():
        acc[...] = jnp.zeros_like(acc)

    p = jnp.concatenate([p_ref[i] for i in range(4)], axis=1)
    acc[...] += dot(p, k_ref[...])

    @pl.when(step == pl.num_programs(0) - 1)
    def _():
        write_partials(acc, out_ref)


def product(present, kernel):
    return call(
        product_body,
        shape((NR, 3, E, U), BF),
        flops=2 * E * 2 * MB,
        moved=5 * MB,
        grid=(NC // 4,),
        in_specs=[
            pl.BlockSpec((4, E, U), lambda i: (i, 0, 0)),
            pl.BlockSpec((4 * U, NR * U), lambda i: (i, 0)),
        ],
        out_specs=pl.BlockSpec((NR, 3, E, U), lambda i: (0, 0, 0, 0)),
        scratch_shapes=[pltpu.VMEM((E, NR * U), F32)],
    )(present, kernel)


def span(b):
    return ((0, 2), (1, 3)) if b == 0 else ((6, 0), (7, 1)) if b == 2 else tuple((2 + i, i) for i in range(4))


def sweep_body(last, own_ref, mid, left, right, inc, tiles, prev, nxt, lefts, rights, meta, moves, *rest):
    if last:
        present_out, field_out, src, srcf, f1 = rest
    else:
        present_out, src, srcf, f1 = rest
        field_out = None
    line = lax.broadcasted_iota(jnp.int32, (S, U), 0).astype(F32)

    def coupling(b):
        m = meta[b].astype(F32)
        return m[0:1], jnp.where(m[1:2] == line, 1.0, 0.0).astype(BF)

    def masked(c, hi, ids):
        return jnp.concatenate([c * jnp.where(hi == float(t), 1.0, 0.0).astype(BF) for t in ids], axis=0)

    for br in range(3):
        for bc in range(3):
            if br == 1 and bc == 1:
                continue
            hi, lo = coupling(3 * br + bc)
            c = (left, mid, right)[bc][br]
            places = [(R * 8 + C, i * 4 + j) for R, i in span(br) for C, j in span(bc)]
            out = dot(masked(c, hi, [t for _, t in places]), lo, NT).astype(BF)
            for n, (w, _) in enumerate(places):
                src[w] = out[n * E : n * E + E]
    hi, lo = coupling(4)
    own = own_ref[...]
    top = own.astype(BF)
    low = (own - top.astype(F32)).astype(BF)
    both = jnp.concatenate([masked(top, hi, range(16)), masked(low, hi, range(16))], axis=0)
    out = dot(both, lo, NT)
    out = out[: 16 * E] + out[16 * E :]
    for t in range(16):
        srcf[t] = out[t * E : t * E + E]
        src[(2 + t // 4) * 8 + 2 + t % 4] = out[t * E : t * E + E].astype(BF)

    def apply(values, base, block, tile, matrix):
        total = None
        for h in range(2):
            ks = (2 * h, 2 * h + 1)
            x = jnp.concatenate([values[base + moves[block, tile * 4 + k]] for k in ks], axis=1)
            a = jnp.concatenate([matrix(k) for k in ks], axis=1)
            y = dot(x, a, NT)
            total = y if total is None else total + y
        return total

    def own_tile(t, carry):
        i, j = t // 4, t % 4
        w = (2 + i) * 8 + 2 + j
        f1[w] = (srcf[t] + apply(src, w - 9, 4, t, lambda k: tiles[t * 4 + k])).astype(BF)
        return carry

    lax.fori_loop(0, 16, own_tile, 0, unroll=2)

    def halo(w, block, tile, ref, start):
        y = apply(src, w - 9, block, tile, lambda k: ref[pl.ds(pl.multiple_of(start + k * S, S), S), :])
        f1[w] = (src[w].astype(F32) + y).astype(BF)

    def edge_row(j, carry):
        halo(8 + 2 + j, 1, 12 + j, prev, j * 4 * S)
        halo(48 + 2 + j, 7, j, nxt, j * 4 * S)
        return carry

    lax.fori_loop(0, 4, edge_row, 0)

    def edge_col(i, carry):
        w = (2 + i) * 8
        halo(w + 1, 3, i * 4 + 3, lefts, (1 + i) * 4 * S)
        halo(w + 6, 5, i * 4, rights, (1 + i) * 4 * S)
        return carry

    lax.fori_loop(0, 4, edge_col, 0)
    halo(9, 0, 15, lefts, 0)
    halo(14, 2, 12, rights, 0)
    halo(49, 6, 3, lefts, 5 * 4 * S)
    halo(54, 8, 0, rights, 5 * 4 * S)

    def final_tile(t, read):
        i, j = t // 4, t % 4
        w = (2 + i) * 8 + 2 + j
        field = srcf[t] + apply(f1, w - 9, 4, t, lambda k: tiles[t * 4 + k])
        if last:
            field_out[t] = field
        a = field.astype(BF)
        b = (field - a.astype(F32)).astype(BF)
        y = dot(jnp.concatenate([a, b], axis=0), lo)
        return read + jnp.where(hi == t.astype(F32), y[:E] + y[E:], 0.0)

    read = lax.fori_loop(0, 16, final_tile, jnp.zeros((E, U), F32), unroll=2)
    present = (inc[...].astype(F32) + read).astype(BF)
    if last:
        present_out[...] = present
    else:
        for c in range(NC):
            present_out[c] = present


def sweep(last, own, mid, left, right, inc, tiles, prev, nxt, lefts, rights, meta, moves):
    vmem = pl.BlockSpec(memory_space=pltpu.VMEM)
    smem = pl.BlockSpec(memory_space=pltpu.SMEM)
    if last:
        out = (shape((E, U), BF), shape((16, E, S), F32))
    else:
        out = shape((NC, E, U), BF)

    def body(*refs):
        sweep_body(last, *refs)

    return call(
        body,
        out,
        flops=2 * E * S * S * 4 * 52,
        moved=6 * MB,
        in_specs=[vmem] * 11 + [smem],
        out_specs=(vmem, vmem) if last else vmem,
        scratch_shapes=[pltpu.VMEM((64, E, S), BF), pltpu.VMEM((16, E, S), F32), pltpu.VMEM((64, E, S), BF)],
    )(own, mid, left, right, inc, tiles, prev, nxt, lefts, rights, meta, moves)


def shift(value, axis):
    size = lax.axis_size(axis)
    up = [(i, i + 1) for i in range(size - 1)]
    return up, [(j, i) for i, j in up]


def per_device(traces, incident, points, coupling, volume_tiles, tile_columns):
    row_up, row_down = shift(None, "row")
    col_up, col_down = shift(None, "col")
    tiles = volume_tiles.reshape(64, S, S)
    rows, cols = pack(traces, points)
    rows = lax.all_to_all(rows, "row", 0, 0, tiled=True)
    cols = lax.all_to_all(cols, "col", 0, 0, tiled=True)

    own_meta = jnp.zeros((16, U), F32)
    own_meta = own_meta.at[0].set((coupling // S).astype(F32)).at[1].set((coupling % S).astype(F32))
    own_meta = own_meta.at[2, :64].set(tile_columns.reshape(64).astype(F32)).astype(BF)
    flat = tiles.reshape(16, 4 * S, S)
    prev = lax.ppermute(jnp.concatenate([flat[12:16].reshape(16 * S, S), own_meta]), "row", row_up)
    nxt = lax.ppermute(jnp.concatenate([flat[0:4].reshape(16 * S, S), own_meta]), "row", row_down)

    def column(j):
        pieces = [prev[j * 4 * S : (j + 1) * 4 * S]] + [flat[4 * i + j] for i in range(4)]
        pieces += [nxt[j * 4 * S : (j + 1) * 4 * S], prev[16 * S :], own_meta, nxt[16 * S :]]
        return jnp.concatenate(pieces)

    lefts = lax.ppermute(column(3), "col", col_up)
    rights = lax.ppermute(column(0), "col", col_down)
    metas = []
    for br in range(3):
        for bc in range(3):
            if bc == 1:
                metas.append((prev[16 * S :], own_meta, nxt[16 * S :])[br])
            else:
                metas.append((lefts if bc == 0 else rights)[24 * S + 16 * br : 24 * S + 16 * br + 16])
    meta = jnp.stack(metas)
    offset = meta[:, 2, :64].astype(jnp.int32)
    moves = offset + 5 * (offset // 3)

    kernel, partials = make_kernel(cols, rows)
    for outer in range(2):
        last = outer == 1
        got = lax.all_to_all(partials, "row", 0, 0, tiled=True)
        sums = jnp.sum(got.astype(F32), axis=0)
        mid = sums.astype(BF)
        left = lax.ppermute(mid, "col", col_up)
        right = lax.ppermute(mid, "col", col_down)
        out = sweep(last, sums[1], mid, left, right, incident, tiles, prev, nxt, lefts, rights, meta, moves)
        if not last:
            partials = product(lax.all_to_all(out, "col", 0, 0, tiled=True), kernel)
    present, field = out
    return present, field.transpose(1, 0, 2).reshape(E, 4, 4, S)


def solution(mesh):
    in_specs = (
        P(None, ("row", "col")),
        P(None, ("row", "col")),
        P(None, ("row", "col")),
        P(("row", "col")),
        P("row", "col", None, None, None),
        P("row", "col", None),
    )
    out_specs = (P(None, ("row", "col")), P(None, "row", "col", None))
    return jax.shard_map(per_device, mesh=mesh, in_specs=in_specs, out_specs=out_specs, check_vma=False)
```

```python
import math

import jax
import jax.numpy as jnp
from jax import lax
from jax.experimental import pallas as pl
from jax.experimental.pallas import tpu as pltpu
from jax.sharding import PartitionSpec as P


E, U, S = 64, 128, 128
NR, NC = 8, 16
TOTAL = U * NR * NC
MB = 1 << 20
ROWS = 4 * S
BF, F32 = jnp.bfloat16, jnp.float32
SIN = (3.14158202, -5.1671428, 2.54189903, -0.55463619)
NT = (((1,), (1,)), ((), ()))
TN = (((0,), (0,)), ((), ()))

SPACING = float(TOTAL) ** (-1.0 / 3.0)
TURNS = 2.0 / SPACING / (2.0 * math.pi)
SMOOTH = (0.5 * SPACING) ** 2 * TURNS * TURNS
FACTOR = TURNS / math.sqrt(2.0 * TOTAL)
WAVE = tuple(c * math.sqrt(2.0 * FACTOR) for c in SIN)


def dot(a, b, dims=(((1,), (0,)), ((), ()))):
    return lax.dot_general(a, b, dims, preferred_element_type=F32)


def call(body, out_shape, *, limit=24 * MB, flops=0, moved=0, **kwargs):
    return pl.pallas_call(
        body,
        out_shape=out_shape,
        compiler_params=pltpu.CompilerParams(vmem_limit_bytes=limit),
        cost_estimate=pl.CostEstimate(flops=flops, bytes_accessed=moved, transcendentals=0),
        **kwargs,
    )


def shape(dims, dtype):
    return jax.ShapeDtypeStruct(dims, dtype)


def hbm(dims, dtype):
    return pltpu.MemorySpace.HBM(dims, dtype)


def vmem(dims, dtype):
    return pltpu.MemorySpace.VMEM(dims, dtype)


def keep(*values):
    return tuple(pltpu.with_memory_space_constraint(v, pltpu.MemorySpace.HBM) for v in values)


IN_VMEM = pl.BlockSpec(memory_space=pltpu.VMEM)
IN_SMEM = pl.BlockSpec(memory_space=pltpu.SMEM)
IN_HBM = pl.BlockSpec(memory_space=pltpu.HBM)
IN_ANY = pl.BlockSpec(memory_space=pl.ANY)


def split3(x):
    a = x.astype(BF).astype(F32)
    b = (x - a).astype(BF).astype(F32)
    return a, b, (x - a - b).astype(BF).astype(F32)


def rows_at(line, pieces):
    out = jnp.zeros((16, U), F32)
    for at, value in pieces:
        out = jnp.where(line == at, value, out)
    return out


def pack_body(traces_h, points_h, coupling_h, columns_h, tiles, row_out, col_out, up, down, meta_out, *scratch):
    traces, points, coupling, columns, sems = scratch
    loads = [(points_h, points), (columns_h, columns), (coupling_h, coupling), (traces_h, traces)]
    loads += [(tiles.at[pl.ds(12 * ROWS, 4 * ROWS)], up.at[pl.ds(0, 4 * ROWS)])]
    loads += [(tiles.at[pl.ds(0, 4 * ROWS)], down.at[pl.ds(0, 4 * ROWS)])]
    loads = [pltpu.make_async_copy(a, b, sems.at[n]) for n, (a, b) in enumerate(loads)]
    for copy in loads:
        copy.start()
    lane = lax.broadcasted_iota(jnp.int32, (1, U), 1)
    loads[0].wait()
    p = (points[...] - 0.5) * TURNS
    parts = split3(p)
    norm = jnp.sum(p * p, axis=0, keepdims=True)
    line = lax.broadcasted_iota(jnp.int32, (16, U), 0)
    source = [(3 * i + d, parts[i][d : d + 1]) for i in range(3) for d in range(3)]
    source += [(9 + i, v) for i, v in enumerate(split3(norm))] + [(12, 1.0)]
    source = rows_at(line, source).astype(BF)
    shifted = split3(norm + SMOOTH)
    target = []
    for j in range(3):
        pieces = [(3 * i + d, -2.0 * parts[j][d : d + 1]) for i in range(3) for d in range(3)]
        if j == 0:
            pieces += [(9 + i, 1.0) for i in range(3)]
        target.append(rows_at(line, pieces + [(12, shifted[j])]).astype(BF))
    for r in range(NR):
        for j in range(3):
            row_out[r, 16 * j : 16 * j + 16] = target[j]
    loads[1].wait()
    offsets = jnp.zeros((1, U), jnp.int32)
    for n in range(64):
        offsets = jnp.where(lane == n, columns[n // 16, n // 4 % 4, n % 4], offsets)
    loads[2].wait()
    at = coupling[...]
    meta = [(0, (at >> 7).astype(F32)), (1, (at & 127).astype(F32)), (2, offsets.astype(F32))]
    meta = rows_at(line, meta).astype(BF)
    meta_out[...] = meta
    up[4 * ROWS :] = meta
    down[4 * ROWS :] = meta
    loads[3].wait()
    for c in range(NC):
        col_out[c, :E] = traces[...]
        col_out[c, E:] = source
    for copy in loads[4:]:
        copy.wait()


def pack(traces, points, coupling, columns, tiles):
    side = hbm((4 * ROWS + 16, S), BF)
    return call(
        pack_body,
        (hbm((NR, 48, U), BF), hbm((NC, E + 16, U), BF), side, side, vmem((16, U), BF)),
        in_specs=[IN_HBM] * 5,
        out_specs=(IN_VMEM,) * 5,
        scratch_shapes=[
            pltpu.VMEM((E, U), BF),
            pltpu.VMEM((3, U), F32),
            pltpu.VMEM((1, U), jnp.int32),
            pltpu.SMEM((4, 4, 4), jnp.int32),
            pltpu.SemaphoreType.DMA((6,)),
        ],
    )(*keep(traces, points, coupling, columns, tiles))


def edge_body(prev, nxt, meta, tiles, left_out, right_out, mid_out, sems):
    copies = []
    for out, j in ((left_out, 3), (right_out, 0)):
        pieces = [prev.at[pl.ds(j * ROWS, ROWS)]]
        pieces += [tiles.at[pl.ds((4 * i + j) * ROWS, ROWS)] for i in range(4)]
        pieces += [nxt.at[pl.ds(j * ROWS, ROWS)]]
        for n, piece in enumerate(pieces):
            copies.append(pltpu.make_async_copy(piece, out.at[pl.ds(n * ROWS, ROWS)], sems.at[len(copies)]))
    for copy in copies:
        copy.start()
    for j in range(3):
        value = (prev, None, nxt)[j]
        value = meta[...] if j == 1 else value[4 * ROWS :]
        for out, start in ((left_out, 6 * ROWS), (right_out, 6 * ROWS), (mid_out, 0)):
            out[start + 16 * j : start + 16 * j + 16] = value
    for copy in copies:
        copy.wait()


def edges(prev, nxt, meta, tiles):
    side = vmem((6 * ROWS + 48, S), BF)
    return call(
        edge_body,
        (side, side, vmem((48, U), BF)),
        moved=4 * MB,
        in_specs=[IN_VMEM, IN_VMEM, IN_VMEM, IN_ANY],
        out_specs=(IN_VMEM,) * 3,
        scratch_shapes=[pltpu.SemaphoreType.DMA((12,))],
    )(prev, nxt, meta, tiles)


def table_body(mid, lefts, rights, meta_out, moves_out, sides, sems):
    copies = [
        pltpu.make_async_copy(h.at[pl.ds(6 * ROWS, 48)], sides.at[n], sems.at[n]) for n, h in enumerate((lefts, rights))
    ]
    for copy in copies:
        copy.start()
    for copy in copies:
        copy.wait()
    moves_out[...] = jnp.zeros_like(moves_out)
    for br in range(3):
        for bc in range(3):
            b = 3 * br + bc
            m = (sides[0], mid[...], sides[1])[bc][16 * br : 16 * br + 16]
            meta_out[16 * b : 16 * b + 16] = m
            o = m.astype(F32)[2:3]
            o = o + 5.0 * (jnp.where(o >= 3.0, 1.0, 0.0) + jnp.where(o >= 6.0, 1.0, 0.0))
            moves_out[b : b + 1] = o.astype(jnp.int32)


def tables(mid, lefts, rights):
    return call(
        table_body,
        (vmem((144, U), BF), vmem((16, U), jnp.int32)),
        in_specs=[IN_VMEM, IN_ANY, IN_ANY],
        out_specs=(IN_VMEM,) * 2,
        scratch_shapes=[pltpu.VMEM((2, 48, U), BF), pltpu.SemaphoreType.DMA((2,))],
    )(mid, lefts, rights)


def write_partials(acc, out):
    for d in range(NR):
        for j in range(3):
            b = d - 1 + j
            if 0 <= b < NR:
                out[d, j] = acc[:, b * U : b * U + U].astype(BF)
            else:
                out[d, j] = jnp.zeros((E, U), BF)


def kernel_body(col_ref, row_ref, k_hbm, out_ref, acc, feats, dist_a, dist_b, k_ref, sem):
    gets = [pltpu.make_async_copy(row_ref.at[r], feats.at[:, pl.ds(r * U, U)], sem) for r in range(NR)]
    for copy in gets:
        copy.start()
    acc[...] = jnp.zeros_like(acc)

    def distances(n, out):
        own = col_ref[n, E:]
        out[...] = dot(jnp.concatenate([own, own, own], axis=0), feats[...], TN)

    def waves(n, dist):
        for i in range(0, U, 16):
            for j in range(0, NR * U, 512):
                d2 = dist[i : i + 16, j : j + 512]
                inv = lax.rsqrt(d2)
                turns = d2 * inv
                f = turns - jnp.round(turns)
                u = f * f
                s = f * (WAVE[0] + u * (WAVE[1] + u * (WAVE[2] + u * WAVE[3])))
                k_ref[n, i : i + 16, j : j + 512] = ((FACTOR - s * s) * inv).astype(BF)

    def accumulate(m):
        p = jnp.concatenate([col_ref[2 * m, :E], col_ref[2 * m + 1, :E]], axis=1)
        k = jnp.concatenate([k_ref[2 * m], k_ref[2 * m + 1]], axis=0)
        acc[...] += dot(p, k)

    def saved(n):
        return pltpu.make_async_copy(k_ref.at[pl.ds(2 * n, 2)], k_hbm.at[pl.ds(2 * n, 2)], sem)

    def pair(m):
        distances(2 * m + 1, dist_b)
        waves(2 * m, dist_a)
        distances(jnp.minimum(2 * m + 2, NC - 1), dist_a)
        waves(2 * m + 1, dist_b)
        saved(m).start()

    for copy in gets:
        copy.wait()
    distances(0, dist_a)
    pair(0)

    def step(m, carry):
        accumulate(m - 1)
        pair(m)
        return carry

    lax.fori_loop(1, NC // 2, step, 0)
    accumulate(NC // 2 - 1)
    write_partials(acc, out_ref)
    pltpu.make_async_copy(k_ref, k_hbm, sem).wait()


def make_kernel(cols, rows):
    return call(
        kernel_body,
        (hbm((NC, U, NR * U), BF), hbm((NR, 3, E, U), BF)),
        flops=40 * 2 * MB,
        moved=6 * MB,
        in_specs=[IN_VMEM, IN_HBM],
        out_specs=(IN_HBM, IN_VMEM),
        scratch_shapes=[
            pltpu.VMEM((E, NR * U), F32),
            pltpu.VMEM((48, NR * U), BF),
            pltpu.VMEM((U, NR * U), F32),
            pltpu.VMEM((U, NR * U), F32),
            pltpu.VMEM((NC, U, NR * U), BF),
            pltpu.SemaphoreType.DMA,
        ],
    )(cols, *keep(rows))


def product_body(p_ref, k_ref, out_ref, acc):
    acc[...] = jnp.zeros_like(acc)
    for n in range(0, NC, 4):
        p = jnp.concatenate([p_ref[n + i] for i in range(4)], axis=1)
        k = jnp.concatenate([k_ref[n + i] for i in range(4)], axis=0)
        acc[...] += dot(p, k)
    write_partials(acc, out_ref)


def product(present, kernel):
    return call(
        product_body,
        shape((NR, 3, E, U), BF),
        flops=2 * E * 2 * MB,
        moved=5 * MB,
        in_specs=[IN_VMEM, IN_VMEM],
        out_specs=IN_VMEM,
        scratch_shapes=[pltpu.VMEM((E, NR * U), F32)],
    )(present, kernel)


def span(b):
    return ((0, 2), (1, 3)) if b == 0 else ((6, 0), (7, 1)) if b == 2 else tuple((2 + i, i) for i in range(4))


def sweep_body(last, own_ref, mid, left, right, inc, metas, moves_v, tiles_h, prev_h, nxt_h, lefts_h, rights_h, *rest):
    if last:
        present_out, field_out = rest[:2]
    else:
        present_out, field_out = rest[0], None
    src, srcf, f1, fields, tiles, prev, nxt, lefts, rights, moves, sems = rest[2 if last else 1 :]
    loads = [(moves_v, moves), (tiles_h, tiles)]
    loads += [(h.at[pl.ds(0, 4 * ROWS)], v) for h, v in ((prev_h, prev), (nxt_h, nxt))]
    loads += [(h.at[pl.ds(0, 6 * ROWS)], v) for h, v in ((lefts_h, lefts), (rights_h, rights))]
    loads = [pltpu.make_async_copy(a, b, sems.at[n]) for n, (a, b) in enumerate(loads)]
    for copy in loads:
        copy.start()
    line = lax.broadcasted_iota(jnp.int32, (S, U), 0).astype(F32)

    def coupling(br, bc):
        at = 16 * (3 * br + bc)
        m = metas[at : at + 16].astype(F32)
        return m[0:1], jnp.where(m[1:2] == line, 1.0, 0.0).astype(BF)

    def masked(c, hi, ids):
        return jnp.concatenate([c * jnp.where(hi == float(t), 1.0, 0.0).astype(BF) for t in ids], axis=0)

    def place(br, bc):
        hi, lo = coupling(br, bc)
        c = (left, mid, right)[bc][br]
        places = [(R * 8 + C, i * 4 + j) for R, i in span(br) for C, j in span(bc)]
        out = dot(masked(c, hi, [t for _, t in places]), lo, NT).astype(BF)
        for n, (w, _) in enumerate(places):
            src[w] = out[n * E : n * E + E]

    hi, lo = coupling(1, 1)
    own = own_ref[...]
    top = own.astype(BF)
    low = (own - top.astype(F32)).astype(BF)
    both = jnp.concatenate([masked(top, hi, range(16)), masked(low, hi, range(16))], axis=1)
    twice = jnp.concatenate([lo, lo], axis=1)
    out = dot(both, twice, NT)
    for t in range(16):
        srcf[t] = out[t * E : t * E + E]
        src[(2 + t // 4) * 8 + 2 + t % 4] = out[t * E : t * E + E].astype(BF)
    for br in range(3):
        for bc in range(3):
            if br != 1 or bc != 1:
                place(br, bc)
    for copy in loads[:2]:
        copy.wait()

    def apply(values, base, block, tile, ref, start):
        total = None
        for h in range(2):
            ks = (2 * h, 2 * h + 1)
            x = jnp.concatenate([values[base + moves[block, tile * 4 + k]] for k in ks], axis=1)
            a = [ref[pl.ds(pl.multiple_of(start + k * S, S), S), :] for k in ks]
            y = dot(x, jnp.concatenate(a, axis=1), NT)
            total = y if total is None else total + y
        return total

    def own_tile(t, carry):
        i, j = t // 4, t % 4
        w = (2 + i) * 8 + 2 + j
        f1[w] = (srcf[t] + apply(src, w - 9, 4, t, tiles, t * ROWS)).astype(BF)
        return carry

    lax.fori_loop(0, 16, own_tile, 0, unroll=4)
    for copy in loads[2:]:
        copy.wait()

    def halo(w, block, tile, ref, start):
        y = apply(src, w - 9, block, tile, ref, start)
        f1[w] = (src[w].astype(F32) + y).astype(BF)

    def edge_row(j, carry):
        halo(8 + 2 + j, 1, 12 + j, prev, j * 4 * S)
        halo(48 + 2 + j, 7, j, nxt, j * 4 * S)
        return carry

    lax.fori_loop(0, 4, edge_row, 0)

    def edge_col(i, carry):
        w = (2 + i) * 8
        halo(w + 1, 3, i * 4 + 3, lefts, (1 + i) * 4 * S)
        halo(w + 6, 5, i * 4, rights, (1 + i) * 4 * S)
        return carry

    lax.fori_loop(0, 4, edge_col, 0)
    halo(9, 0, 15, lefts, 0)
    halo(14, 2, 12, rights, 0)
    halo(49, 6, 3, lefts, 5 * 4 * S)
    halo(54, 8, 0, rights, 5 * 4 * S)

    def final_tile(t, carry):
        i, j = t // 4, t % 4
        w = (2 + i) * 8 + 2 + j
        field = srcf[t] + apply(f1, w - 9, 4, t, tiles, t * ROWS)
        if last:
            field_out[pl.ds(t, E, stride=16), :] = field
        a = field.astype(BF)
        fields[t, :, :S] = a
        fields[t, :, S:] = (field - a.astype(F32)).astype(BF)
        return carry

    lax.fori_loop(0, 16, final_tile, 0, unroll=4)
    y = dot(fields[...].reshape(16 * E, 2 * S), jnp.concatenate([lo, lo], axis=0))
    read = jnp.zeros((E, U), F32)
    for t in range(16):
        read += jnp.where(hi == float(t), y[t * E : t * E + E], 0.0)
    present = (inc[...].astype(F32) + read).astype(BF)
    if last:
        present_out[...] = present
    else:
        for c in range(NC):
            present_out[c] = present


def sweep(last, *args):
    if last:
        out = (shape((E, U), BF), shape((E * 16, S), F32))
    else:
        out = shape((NC, E, U), BF)

    def body(*refs):
        sweep_body(last, *refs)

    return call(
        body,
        out,
        flops=2 * E * S * S * 4 * 52,
        moved=6 * MB,
        in_specs=[IN_VMEM] * 7 + [IN_HBM] * 5,
        out_specs=(IN_VMEM, IN_VMEM) if last else IN_VMEM,
        scratch_shapes=[
            pltpu.VMEM((64, E, S), BF),
            pltpu.VMEM((16, E, S), F32),
            pltpu.VMEM((64, E, S), BF),
            pltpu.VMEM((16, E, 2 * S), BF),
            pltpu.VMEM((16 * ROWS, S), BF),
            pltpu.VMEM((4 * ROWS, S), BF),
            pltpu.VMEM((4 * ROWS, S), BF),
            pltpu.VMEM((6 * ROWS, S), BF),
            pltpu.VMEM((6 * ROWS, S), BF),
            pltpu.SMEM((16, U), jnp.int32),
            pltpu.SemaphoreType.DMA((6,)),
        ],
    )(*args[:7], *keep(*args[7:]))


def shift(axis):
    size = lax.axis_size(axis)
    up = [(i, i + 1) for i in range(size - 1)]
    return up, [(j, i) for i, j in up]


def per_device(traces, incident, points, coupling, volume_tiles, tile_columns):
    row_up, row_down = shift("row")
    col_up, col_down = shift("col")
    tiles = volume_tiles.reshape(16 * ROWS, S)
    rows, cols, up, down, meta = pack(traces, points, coupling.reshape(1, U), tile_columns, tiles)
    rows = lax.all_to_all(rows, "row", 0, 0, tiled=True)
    cols = lax.all_to_all(cols, "col", 0, 0, tiled=True)
    prev = lax.ppermute(up, "row", row_up)
    nxt = lax.ppermute(down, "row", row_down)
    kernel, partials = make_kernel(cols, rows)
    lefts, rights, mid = edges(prev, nxt, meta, tiles)
    lefts = lax.ppermute(lefts, "col", col_up)
    rights = lax.ppermute(rights, "col", col_down)
    metas, moves = tables(mid, lefts, rights)
    for outer in range(2):
        last = outer == 1
        got = lax.all_to_all(partials, "row", 0, 0, tiled=True)
        sums = jnp.sum(got.astype(F32), axis=0)
        mid = sums.astype(BF)
        left = lax.ppermute(mid, "col", col_up)
        right = lax.ppermute(mid, "col", col_down)
        out = sweep(last, sums[1], mid, left, right, incident, metas, moves, tiles, prev, nxt, lefts, rights)
        if not last:
            out = lax.all_to_all(out, "col", 0, 0, tiled=True)
            partials = product(out, kernel)
    present, field = out
    return present, field.reshape(E, 4, 4, S)


def solution(mesh):
    in_specs = (
        P(None, ("row", "col")),
        P(None, ("row", "col")),
        P(None, ("row", "col")),
        P(("row", "col")),
        P("row", "col", None, None, None),
        P("row", "col", None),
    )
    out_specs = (P(None, ("row", "col")), P(None, "row", "col", None))
    return jax.shard_map(per_device, mesh=mesh, in_specs=in_specs, out_specs=out_specs, check_vma=False)
```

```python
import math

import jax
import jax.numpy as jnp
from jax import lax
from jax.experimental import pallas as pl
from jax.experimental.pallas import tpu as pltpu
from jax.sharding import PartitionSpec as P


E, U, S = 64, 128, 128
NR, NC = 8, 16
TOTAL = U * NR * NC
MB = 1 << 20
HEAD = 3 * E
ROWS = 4 * S
TAIL = HEAD + 2 * ROWS
BF, F32 = jnp.bfloat16, jnp.float32
SIN = (3.14158202, -5.1671428, 2.54189903, -0.55463619)
NT = (((1,), (1,)), ((), ()))
TN = (((0,), (0,)), ((), ()))

SPACING = float(TOTAL) ** (-1.0 / 3.0)
TURNS = 2.0 / SPACING / (2.0 * math.pi)
SMOOTH = (0.5 * SPACING) ** 2 * TURNS * TURNS
FACTOR = TURNS / math.sqrt(2.0 * TOTAL)
WAVE = tuple(c * math.sqrt(2.0 * FACTOR) for c in SIN)


def dot(a, b, dims=(((1,), (0,)), ((), ()))):
    return lax.dot_general(a, b, dims, preferred_element_type=F32)


def call(body, out_shape, *, limit=24 * MB, flops=0, moved=0, **kwargs):
    return pl.pallas_call(
        body,
        out_shape=out_shape,
        compiler_params=pltpu.CompilerParams(vmem_limit_bytes=limit),
        cost_estimate=pl.CostEstimate(flops=flops, bytes_accessed=moved, transcendentals=0),
        **kwargs,
    )


def shape(dims, dtype):
    return jax.ShapeDtypeStruct(dims, dtype)


def hbm(dims, dtype):
    return pltpu.MemorySpace.HBM(dims, dtype)


def vmem(dims, dtype):
    return pltpu.MemorySpace.VMEM(dims, dtype)


def keep(*values):
    return tuple(pltpu.with_memory_space_constraint(v, pltpu.MemorySpace.HBM) for v in values)


IN_VMEM = pl.BlockSpec(memory_space=pltpu.VMEM)
IN_SMEM = pl.BlockSpec(memory_space=pltpu.SMEM)
IN_HBM = pl.BlockSpec(memory_space=pltpu.HBM)
IN_ANY = pl.BlockSpec(memory_space=pl.ANY)


def split3(x):
    a = x.astype(BF).astype(F32)
    b = (x - a).astype(BF).astype(F32)
    return a, b, (x - a - b).astype(BF).astype(F32)


def rows_at(line, pieces):
    out = jnp.zeros((16, U), F32)
    for at, value in pieces:
        out = jnp.where(line == at, value, out)
    return out


def pack_body(traces_h, points_h, coupling_h, columns_h, tiles, row_out, col_out, up, down, meta_out, *scratch):
    traces, points, coupling, columns, sems = scratch
    loads = [(points_h, points), (columns_h, columns), (coupling_h, coupling), (traces_h, traces)]
    loads += [(tiles.at[pl.ds(12 * ROWS, 4 * ROWS)], up.at[pl.ds(0, 4 * ROWS)])]
    loads += [(tiles.at[pl.ds(0, 4 * ROWS)], down.at[pl.ds(0, 4 * ROWS)])]
    loads = [pltpu.make_async_copy(a, b, sems.at[n]) for n, (a, b) in enumerate(loads)]
    for copy in loads:
        copy.start()
    lane = lax.broadcasted_iota(jnp.int32, (1, U), 1)
    loads[0].wait()
    p = (points[...] - 0.5) * TURNS
    parts = split3(p)
    norm = jnp.sum(p * p, axis=0, keepdims=True)
    line = lax.broadcasted_iota(jnp.int32, (16, U), 0)
    source = [(3 * i + d, parts[i][d : d + 1]) for i in range(3) for d in range(3)]
    source += [(9 + i, v) for i, v in enumerate(split3(norm))] + [(12, 1.0)]
    source = rows_at(line, source).astype(BF)
    shifted = split3(norm + SMOOTH)
    target = []
    for j in range(3):
        pieces = [(3 * i + d, -2.0 * parts[j][d : d + 1]) for i in range(3) for d in range(3)]
        if j == 0:
            pieces += [(9 + i, 1.0) for i in range(3)]
        target.append(rows_at(line, pieces + [(12, shifted[j])]).astype(BF))
    for r in range(NR):
        for j in range(3):
            row_out[r, 16 * j : 16 * j + 16] = target[j]
    loads[1].wait()
    offsets = jnp.zeros((1, U), jnp.int32)
    for n in range(64):
        offsets = jnp.where(lane == n, columns[n // 16, n // 4 % 4, n % 4], offsets)
    loads[2].wait()
    at = coupling[...]
    meta = [(0, (at >> 7).astype(F32)), (1, (at & 127).astype(F32)), (2, offsets.astype(F32))]
    meta = rows_at(line, meta).astype(BF)
    meta_out[...] = meta
    up[4 * ROWS :] = meta
    down[4 * ROWS :] = meta
    loads[3].wait()
    for c in range(NC):
        col_out[c, :E] = traces[...]
        col_out[c, E:] = source
    for copy in loads[4:]:
        copy.wait()


def pack(traces, points, coupling, columns, tiles):
    side = hbm((4 * ROWS + 16, S), BF)
    return call(
        pack_body,
        (hbm((NR, 48, U), BF), hbm((NC, E + 16, U), BF), side, side, vmem((16, U), BF)),
        in_specs=[IN_HBM] * 5,
        out_specs=(IN_VMEM,) * 5,
        scratch_shapes=[
            pltpu.VMEM((E, U), BF),
            pltpu.VMEM((3, U), F32),
            pltpu.VMEM((1, U), jnp.int32),
            pltpu.SMEM((4, 4, 4), jnp.int32),
            pltpu.SemaphoreType.DMA((6,)),
        ],
    )(*keep(traces, points, coupling, columns, tiles))


def fill_body(tiles, left_out, right_out, sems):
    copies = []
    for out, j in ((left_out, 3), (right_out, 0)):
        for i in range(4):
            piece = tiles.at[pl.ds((4 * i + j) * ROWS, ROWS)]
            copies.append(pltpu.make_async_copy(piece, out.at[pl.ds(i * ROWS, ROWS)], sems.at[len(copies)]))
    for copy in copies:
        copy.start()
    for copy in copies:
        copy.wait()


def fill(tiles):
    side = shape((4 * ROWS, S), BF)
    return call(
        fill_body,
        (side, side),
        moved=2 * MB,
        in_specs=[IN_HBM],
        out_specs=(IN_VMEM,) * 2,
        scratch_shapes=[pltpu.SemaphoreType.DMA((8,))],
    )(*keep(tiles))


def near_body(got, prev, nxt, meta, own_out, mid_out, left_out, right_out, meta_out, sems):
    copies = []
    for out, j in ((left_out, 3), (right_out, 0)):
        for n, source in enumerate((prev, nxt)):
            piece = source.at[pl.ds(j * ROWS, ROWS)]
            copies.append(pltpu.make_async_copy(piece, out.at[pl.ds(HEAD + n * ROWS, ROWS)], sems.at[len(copies)]))
    for n, source in enumerate((prev, nxt)):
        piece = source.at[pl.ds(4 * ROWS, 16)]
        copies.append(pltpu.make_async_copy(piece, meta_out.at[pl.ds(32 * n, 16)], sems.at[len(copies)]))
    for copy in copies:
        copy.start()
    meta_out[16:32] = meta[...]
    for j in range(3):
        total = got[0, j].astype(F32)
        for r in range(1, NR):
            total += got[r, j].astype(F32)
        if j == 1:
            own_out[...] = total
        value = total.astype(BF)
        mid_out[j * E : j * E + E] = value
        left_out[j * E : j * E + E] = value
        right_out[j * E : j * E + E] = value
    for copy in copies:
        copy.wait()
    metas = meta_out[...]
    left_out[TAIL:] = metas
    right_out[TAIL:] = metas


def near(got, prev, nxt, meta):
    side = shape((TAIL + 48, S), BF)
    return call(
        near_body,
        (shape((E, U), F32), shape((HEAD, U), BF), side, side, shape((48, U), BF)),
        moved=2 * MB,
        in_specs=[IN_VMEM, IN_ANY, IN_ANY, IN_VMEM],
        out_specs=(IN_VMEM,) * 5,
        scratch_shapes=[pltpu.SemaphoreType.DMA((6,))],
    )(got, prev, nxt, meta)


def write_partials(acc, out):
    for d in range(NR):
        for j in range(3):
            b = d - 1 + j
            if 0 <= b < NR:
                out[d, j] = acc[:, b * U : b * U + U].astype(BF)
            else:
                out[d, j] = jnp.zeros((E, U), BF)


def kernel_body(col_ref, row_ref, k_hbm, out_ref, acc, feats, dist_a, dist_b, k_ref, sem):
    gets = [pltpu.make_async_copy(row_ref.at[r], feats.at[:, pl.ds(r * U, U)], sem) for r in range(NR)]
    for copy in gets:
        copy.start()
    acc[...] = jnp.zeros_like(acc)

    def distances(n, out):
        own = col_ref[n, E:]
        out[...] = dot(jnp.concatenate([own, own, own], axis=0), feats[...], TN)

    def waves(n, dist):
        for i in range(0, U, 16):
            for j in range(0, NR * U, 512):
                d2 = dist[i : i + 16, j : j + 512]
                inv = lax.rsqrt(d2)
                turns = d2 * inv
                f = turns - jnp.round(turns)
                u = f * f
                s = f * (WAVE[0] + u * (WAVE[1] + u * (WAVE[2] + u * WAVE[3])))
                k_ref[n, i : i + 16, j : j + 512] = ((FACTOR - s * s) * inv).astype(BF)

    def accumulate(m):
        p = jnp.concatenate([col_ref[2 * m, :E], col_ref[2 * m + 1, :E]], axis=1)
        k = jnp.concatenate([k_ref[2 * m], k_ref[2 * m + 1]], axis=0)
        acc[...] += dot(p, k)

    def saved(n):
        return pltpu.make_async_copy(k_ref.at[pl.ds(2 * n, 2)], k_hbm.at[pl.ds(2 * n, 2)], sem)

    def pair(m):
        distances(2 * m + 1, dist_b)
        waves(2 * m, dist_a)
        distances(jnp.minimum(2 * m + 2, NC - 1), dist_a)
        waves(2 * m + 1, dist_b)
        saved(m).start()

    for copy in gets:
        copy.wait()
    distances(0, dist_a)
    pair(0)

    def step(m, carry):
        accumulate(m - 1)
        pair(m)
        return carry

    lax.fori_loop(1, NC // 2, step, 0)
    accumulate(NC // 2 - 1)
    write_partials(acc, out_ref)
    pltpu.make_async_copy(k_ref, k_hbm, sem).wait()


def make_kernel(cols, rows):
    return call(
        kernel_body,
        (hbm((NC, U, NR * U), BF), hbm((NR, 3, E, U), BF)),
        flops=40 * 2 * MB,
        moved=6 * MB,
        in_specs=[IN_VMEM, IN_HBM],
        out_specs=(IN_HBM, IN_VMEM),
        scratch_shapes=[
            pltpu.VMEM((E, NR * U), F32),
            pltpu.VMEM((48, NR * U), BF),
            pltpu.VMEM((U, NR * U), F32),
            pltpu.VMEM((U, NR * U), F32),
            pltpu.VMEM((NC, U, NR * U), BF),
            pltpu.SemaphoreType.DMA,
        ],
    )(cols, *keep(rows))


def product_body(p_ref, k_ref, out_ref, acc):
    acc[...] = jnp.zeros_like(acc)
    for n in range(0, NC, 4):
        p = jnp.concatenate([p_ref[n + i] for i in range(4)], axis=1)
        k = jnp.concatenate([k_ref[n + i] for i in range(4)], axis=0)
        acc[...] += dot(p, k)
    write_partials(acc, out_ref)


def product(present, kernel):
    return call(
        product_body,
        shape((NR, 3, E, U), BF),
        flops=2 * E * 2 * MB,
        moved=5 * MB,
        in_specs=[IN_VMEM, IN_VMEM],
        out_specs=IN_VMEM,
        scratch_shapes=[pltpu.VMEM((E, NR * U), F32)],
    )(present, kernel)


def span(b):
    return ((0, 2), (1, 3)) if b == 0 else ((6, 0), (7, 1)) if b == 2 else tuple((2 + i, i) for i in range(4))


def sweep_body(last, own_ref, mid, left, right, left_far, right_far, inc, mid_metas, tiles_h, prev_h, nxt_h, lefts_h, rights_h, *rest):
    if last:
        present_out, field_out = rest[:2]
    else:
        present_out, field_out = rest[0], None
    src, srcf, f1, fields, tiles, prev, nxt, lefts, rights, moves_v, moves, sems = rest[2 if last else 1 :]
    loads = [(moves_v, moves), (tiles_h, tiles)]
    loads += [(h.at[pl.ds(0, 4 * ROWS)], v) for h, v in ((prev_h, prev), (nxt_h, nxt))]
    loads += [(lefts_h, lefts), (rights_h, rights)]
    loads = [pltpu.make_async_copy(a, b, sems.at[n]) for n, (a, b) in enumerate(loads)]
    for copy in loads[1:]:
        copy.start()

    def meta(br, bc):
        m = mid_metas[16 * br : 16 * br + 16] if bc == 1 else (left_far, right_far)[bc // 2][TAIL + 16 * br : TAIL + 16 * br + 16]
        return m.astype(F32)

    moves_v[...] = jnp.zeros_like(moves_v)
    for br in range(3):
        for bc in range(3):
            o = meta(br, bc)[2:3]
            o = o + 5.0 * (jnp.where(o >= 3.0, 1.0, 0.0) + jnp.where(o >= 6.0, 1.0, 0.0))
            moves_v[3 * br + bc : 3 * br + bc + 1] = o.astype(jnp.int32)
    loads[0].start()
    line = lax.broadcasted_iota(jnp.int32, (S, U), 0).astype(F32)

    def coupling(br, bc):
        m = meta(br, bc)
        return m[0:1], jnp.where(m[1:2] == line, 1.0, 0.0).astype(BF)

    def masked(c, hi, ids):
        return jnp.concatenate([c * jnp.where(hi == float(t), 1.0, 0.0).astype(BF) for t in ids], axis=0)

    def place(br, bc):
        hi, lo = coupling(br, bc)
        c = (left, mid, right)[bc][br * E : br * E + E]
        places = [(R * 8 + C, i * 4 + j) for R, i in span(br) for C, j in span(bc)]
        out = dot(masked(c, hi, [t for _, t in places]), lo, NT).astype(BF)
        for n, (w, _) in enumerate(places):
            src[w] = out[n * E : n * E + E]

    hi, lo = coupling(1, 1)
    own = own_ref[...]
    top = own.astype(BF)
    low = (own - top.astype(F32)).astype(BF)
    both = jnp.concatenate([masked(top, hi, range(16)), masked(low, hi, range(16))], axis=1)
    twice = jnp.concatenate([lo, lo], axis=1)
    out = dot(both, twice, NT)
    for t in range(16):
        srcf[t] = out[t * E : t * E + E]
        src[(2 + t // 4) * 8 + 2 + t % 4] = out[t * E : t * E + E].astype(BF)
    for br in range(3):
        for bc in range(3):
            if br != 1 or bc != 1:
                place(br, bc)
    for copy in loads[:2]:
        copy.wait()

    def apply(values, base, block, tile, ref, start):
        total = None
        for h in range(2):
            ks = (2 * h, 2 * h + 1)
            x = jnp.concatenate([values[base + moves[block, tile * 4 + k]] for k in ks], axis=1)
            a = [ref[pl.ds(pl.multiple_of(start + k * S, 64), S), :] for k in ks]
            y = dot(x, jnp.concatenate(a, axis=1), NT)
            total = y if total is None else total + y
        return total

    def own_tile(t, carry):
        i, j = t // 4, t % 4
        w = (2 + i) * 8 + 2 + j
        f1[w] = (srcf[t] + apply(src, w - 9, 4, t, tiles, t * ROWS)).astype(BF)
        return carry

    lax.fori_loop(0, 16, own_tile, 0, unroll=4)
    for copy in loads[2:]:
        copy.wait()

    def halo(w, block, tile, ref, start):
        y = apply(src, w - 9, block, tile, ref, start)
        f1[w] = (src[w].astype(F32) + y).astype(BF)

    def edge_row(j, carry):
        halo(8 + 2 + j, 1, 12 + j, prev, j * 4 * S)
        halo(48 + 2 + j, 7, j, nxt, j * 4 * S)
        return carry

    lax.fori_loop(0, 4, edge_row, 0)

    def edge_col(i, carry):
        w = (2 + i) * 8
        halo(w + 1, 3, i * 4 + 3, lefts, i * ROWS)
        halo(w + 6, 5, i * 4, rights, i * ROWS)
        return carry

    lax.fori_loop(0, 4, edge_col, 0)
    halo(9, 0, 15, left_far, HEAD)
    halo(14, 2, 12, right_far, HEAD)
    halo(49, 6, 3, left_far, HEAD + ROWS)
    halo(54, 8, 0, right_far, HEAD + ROWS)

    def final_tile(t, carry):
        i, j = t // 4, t % 4
        w = (2 + i) * 8 + 2 + j
        field = srcf[t] + apply(f1, w - 9, 4, t, tiles, t * ROWS)
        if last:
            field_out[pl.ds(t, E, stride=16), :] = field
        a = field.astype(BF)
        fields[t, :, :S] = a
        fields[t, :, S:] = (field - a.astype(F32)).astype(BF)
        return carry

    lax.fori_loop(0, 16, final_tile, 0, unroll=4)
    y = dot(fields[...].reshape(16 * E, 2 * S), jnp.concatenate([lo, lo], axis=0))
    read = jnp.zeros((E, U), F32)
    for t in range(16):
        read += jnp.where(hi == float(t), y[t * E : t * E + E], 0.0)
    present = (inc[...].astype(F32) + read).astype(BF)
    if last:
        present_out[...] = present
    else:
        for c in range(NC):
            present_out[c] = present


def sweep(last, *args):
    if last:
        out = (shape((E, U), BF), shape((E * 16, S), F32))
    else:
        out = shape((NC, E, U), BF)

    def body(*refs):
        sweep_body(last, *refs)

    return call(
        body,
        out,
        flops=2 * E * S * S * 4 * 52,
        moved=6 * MB,
        in_specs=[IN_VMEM] * 8 + [IN_HBM] * 5,
        out_specs=(IN_VMEM, IN_VMEM) if last else IN_VMEM,
        scratch_shapes=[
            pltpu.VMEM((64, E, S), BF),
            pltpu.VMEM((16, E, S), F32),
            pltpu.VMEM((64, E, S), BF),
            pltpu.VMEM((16, E, 2 * S), BF),
            pltpu.VMEM((16 * ROWS, S), BF),
            pltpu.VMEM((4 * ROWS, S), BF),
            pltpu.VMEM((4 * ROWS, S), BF),
            pltpu.VMEM((4 * ROWS, S), BF),
            pltpu.VMEM((4 * ROWS, S), BF),
            pltpu.VMEM((16, U), jnp.int32),
            pltpu.SMEM((16, U), jnp.int32),
            pltpu.SemaphoreType.DMA((6,)),
        ],
    )(*args[:8], *keep(*args[8:]))


def shift(axis):
    size = lax.axis_size(axis)
    up = [(i, i + 1) for i in range(size - 1)]
    return up, [(j, i) for i, j in up]


def per_device(traces, incident, points, coupling, volume_tiles, tile_columns):
    row_up, row_down = shift("row")
    col_up, col_down = shift("col")
    tiles = volume_tiles.reshape(16 * ROWS, S)
    rows, cols, up, down, meta = pack(traces, points, coupling.reshape(1, U), tile_columns, tiles)
    rows = lax.all_to_all(rows, "row", 0, 0, tiled=True)
    cols = lax.all_to_all(cols, "col", 0, 0, tiled=True)
    lefts, rights = fill(tiles)
    lefts = lax.ppermute(lefts, "col", col_up)
    rights = lax.ppermute(rights, "col", col_down)
    prev = lax.ppermute(up, "row", row_up)
    nxt = lax.ppermute(down, "row", row_down)
    kernel, partials = make_kernel(cols, rows)
    got = lax.all_to_all(partials, "row", 0, 0, tiled=True)
    own, mid, to_right, to_left, metas = near(got, prev, nxt, meta)
    left = lax.ppermute(to_right, "col", col_up)
    right = lax.ppermute(to_left, "col", col_down)
    far = (left, right)
    for outer in range(2):
        last = outer == 1
        out = sweep(last, own, mid, left, right, *far, incident, metas, tiles, prev, nxt, lefts, rights)
        if not last:
            out = lax.all_to_all(out, "col", 0, 0, tiled=True)
            partials = product(out, kernel)
            got = lax.all_to_all(partials, "row", 0, 0, tiled=True)
            sums = jnp.sum(got.astype(F32), axis=0)
            own, mid = sums[1], sums.astype(BF).reshape(HEAD, U)
            left = lax.ppermute(mid, "col", col_up)
            right = lax.ppermute(mid, "col", col_down)
    present, field = out
    return present, field.reshape(E, 4, 4, S)


def solution(mesh):
    in_specs = (
        P(None, ("row", "col")),
        P(None, ("row", "col")),
        P(None, ("row", "col")),
        P(("row", "col")),
        P("row", "col", None, None, None),
        P("row", "col", None),
    )
    out_specs = (P(None, ("row", "col")), P(None, "row", "col", None))
    return jax.shard_map(per_device, mesh=mesh, in_specs=in_specs, out_specs=out_specs, check_vma=False)
```

```python
import math

import jax
import jax.numpy as jnp
from jax import lax
from jax.experimental import pallas as pl
from jax.experimental.pallas import tpu as pltpu
from jax.sharding import PartitionSpec as P


E, U, S = 64, 128, 128
NR, NC = 8, 16
TOTAL = U * NR * NC
MB = 1 << 20
HEAD = 3 * E
ROWS = 4 * S
TAIL = HEAD + 2 * ROWS
BF, F32 = jnp.bfloat16, jnp.float32
SIN = (3.14158202, -5.1671428, 2.54189903, -0.55463619)
NT = (((1,), (1,)), ((), ()))
TN = (((0,), (0,)), ((), ()))

SPACING = float(TOTAL) ** (-1.0 / 3.0)
TURNS = 2.0 / SPACING / (2.0 * math.pi)
SMOOTH = (0.5 * SPACING) ** 2 * TURNS * TURNS
FACTOR = TURNS / math.sqrt(2.0 * TOTAL)
WAVE = tuple(c * math.sqrt(2.0 * FACTOR) for c in SIN)


def dot(a, b, dims=(((1,), (0,)), ((), ()))):
    return lax.dot_general(a, b, dims, preferred_element_type=F32)


def call(body, out_shape, *, limit=24 * MB, flops=0, moved=0, **kwargs):
    return pl.pallas_call(
        body,
        out_shape=out_shape,
        compiler_params=pltpu.CompilerParams(vmem_limit_bytes=limit),
        cost_estimate=pl.CostEstimate(flops=flops, bytes_accessed=moved, transcendentals=0),
        **kwargs,
    )


def shape(dims, dtype):
    return jax.ShapeDtypeStruct(dims, dtype)


def hbm(dims, dtype):
    return pltpu.MemorySpace.HBM(dims, dtype)


def vmem(dims, dtype):
    return pltpu.MemorySpace.VMEM(dims, dtype)


def keep(*values):
    return tuple(pltpu.with_memory_space_constraint(v, pltpu.MemorySpace.HBM) for v in values)


IN_VMEM = pl.BlockSpec(memory_space=pltpu.VMEM)
IN_SMEM = pl.BlockSpec(memory_space=pltpu.SMEM)
IN_HBM = pl.BlockSpec(memory_space=pltpu.HBM)
IN_ANY = pl.BlockSpec(memory_space=pl.ANY)


def split3(x):
    a = x.astype(BF).astype(F32)
    b = (x - a).astype(BF).astype(F32)
    return a, b, (x - a - b).astype(BF).astype(F32)


def rows_at(line, pieces):
    out = jnp.zeros((16, U), F32)
    for at, value in pieces:
        out = jnp.where(line == at, value, out)
    return out


def pack_body(traces_h, points_h, coupling_h, columns_h, tiles, row_out, col_out, up, down, meta_out, *scratch):
    traces, points, coupling, columns, sems = scratch
    loads = [(points_h, points), (columns_h, columns), (coupling_h, coupling), (traces_h, traces)]
    loads += [(tiles.at[pl.ds(12 * ROWS, 4 * ROWS)], up.at[pl.ds(0, 4 * ROWS)])]
    loads += [(tiles.at[pl.ds(0, 4 * ROWS)], down.at[pl.ds(0, 4 * ROWS)])]
    loads = [pltpu.make_async_copy(a, b, sems.at[n]) for n, (a, b) in enumerate(loads)]
    for copy in loads:
        copy.start()
    lane = lax.broadcasted_iota(jnp.int32, (1, U), 1)
    loads[0].wait()
    p = (points[...] - 0.5) * TURNS
    parts = split3(p)
    norm = jnp.sum(p * p, axis=0, keepdims=True)
    line = lax.broadcasted_iota(jnp.int32, (16, U), 0)
    source = [(3 * i + d, parts[i][d : d + 1]) for i in range(3) for d in range(3)]
    source += [(9 + i, v) for i, v in enumerate(split3(norm))] + [(12, 1.0)]
    source = rows_at(line, source).astype(BF)
    shifted = split3(norm + SMOOTH)
    target = []
    for j in range(3):
        pieces = [(3 * i + d, -2.0 * parts[j][d : d + 1]) for i in range(3) for d in range(3)]
        if j == 0:
            pieces += [(9 + i, 1.0) for i in range(3)]
        target.append(rows_at(line, pieces + [(12, shifted[j])]).astype(BF))
    for r in range(NR):
        for j in range(3):
            row_out[r, 16 * j : 16 * j + 16] = target[j]
    loads[1].wait()
    offsets = jnp.zeros((1, U), jnp.int32)
    for n in range(64):
        offsets = jnp.where(lane == n, columns[n // 16, n // 4 % 4, n % 4], offsets)
    loads[2].wait()
    at = coupling[...]
    meta = [(0, (at >> 7).astype(F32)), (1, (at & 127).astype(F32)), (2, offsets.astype(F32))]
    meta = rows_at(line, meta).astype(BF)
    meta_out[...] = meta
    up[4 * ROWS :] = meta
    down[4 * ROWS :] = meta
    loads[3].wait()
    for c in range(NC):
        col_out[c, :E] = traces[...]
        col_out[c, E:] = source
    for copy in loads[4:]:
        copy.wait()


def pack(traces, points, coupling, columns, tiles):
    side = hbm((4 * ROWS + 16, S), BF)
    return call(
        pack_body,
        (hbm((NR, 48, U), BF), hbm((NC, E + 16, U), BF), side, side, vmem((16, U), BF)),
        in_specs=[IN_HBM] * 5,
        out_specs=(IN_VMEM,) * 5,
        scratch_shapes=[
            pltpu.VMEM((E, U), BF),
            pltpu.VMEM((3, U), F32),
            pltpu.VMEM((1, U), jnp.int32),
            pltpu.SMEM((4, 4, 4), jnp.int32),
            pltpu.SemaphoreType.DMA((6,)),
        ],
    )(*keep(traces, points, coupling, columns, tiles))


def column_of(odd, side):
    return 3 * odd if side else 3 - 3 * odd


def fill_body(tiles, left_out, right_out, sems):
    copies = []
    for out, j in ((left_out, 3), (right_out, 0)):
        for i in range(4):
            piece = tiles.at[pl.ds((4 * i + j) * ROWS, ROWS)]
            copies.append(pltpu.make_async_copy(piece, out.at[pl.ds(i * ROWS, ROWS)], sems.at[len(copies)]))
    for copy in copies:
        copy.start()
    for copy in copies:
        copy.wait()


def fill(tiles):
    side = shape((4 * ROWS, S), BF)
    return call(
        fill_body,
        (side, side),
        moved=2 * MB,
        in_specs=[IN_HBM],
        out_specs=(IN_VMEM,) * 2,
        scratch_shapes=[pltpu.SemaphoreType.DMA((8,))],
    )(*keep(tiles))


def near_body(parity, got, prev, nxt, meta, own_out, mid_out, out_a, out_b, meta_out, sems):
    copies = []
    for side, out in enumerate((out_a, out_b)):
        j = column_of(parity[0], side)
        for n, source in enumerate((prev, nxt)):
            piece = source.at[pl.ds(pl.multiple_of(j * ROWS, ROWS), ROWS)]
            copies.append(pltpu.make_async_copy(piece, out.at[pl.ds(HEAD + n * ROWS, ROWS)], sems.at[len(copies)]))
    for n, source in enumerate((prev, nxt)):
        piece = source.at[pl.ds(4 * ROWS, 16)]
        copies.append(pltpu.make_async_copy(piece, meta_out.at[pl.ds(32 * n, 16)], sems.at[len(copies)]))
    for copy in copies:
        copy.start()
    meta_out[16:32] = meta[...]
    for j in range(3):
        total = got[0, j].astype(F32)
        for r in range(1, NR):
            total += got[r, j].astype(F32)
        if j == 1:
            own_out[...] = total
        value = total.astype(BF)
        mid_out[j * E : j * E + E] = value
        out_a[j * E : j * E + E] = value
        out_b[j * E : j * E + E] = value
    for copy in copies:
        copy.wait()
    metas = meta_out[...]
    out_a[TAIL:] = metas
    out_b[TAIL:] = metas


def near(parity, got, prev, nxt, meta):
    side = shape((TAIL + 48, S), BF)
    return call(
        near_body,
        (shape((E, U), F32), shape((HEAD, U), BF), side, side, shape((48, U), BF)),
        moved=2 * MB,
        in_specs=[IN_SMEM, IN_VMEM, IN_ANY, IN_ANY, IN_VMEM],
        out_specs=(IN_VMEM,) * 5,
        scratch_shapes=[pltpu.SemaphoreType.DMA((6,))],
    )(parity, got, prev, nxt, meta)


def write_partials(acc, out):
    for d in range(NR):
        for j in range(3):
            b = d - 1 + j
            if 0 <= b < NR:
                out[d, j] = acc[:, b * U : b * U + U].astype(BF)
            else:
                out[d, j] = jnp.zeros((E, U), BF)


def kernel_body(col_ref, row_ref, k_hbm, out_ref, acc, feats, dist_a, dist_b, k_ref, sem):
    gets = [pltpu.make_async_copy(row_ref.at[r], feats.at[:, pl.ds(r * U, U)], sem) for r in range(NR)]
    for copy in gets:
        copy.start()
    acc[...] = jnp.zeros_like(acc)

    def distances(n, out):
        own = col_ref[n, E:]
        out[...] = dot(jnp.concatenate([own, own, own], axis=0), feats[...], TN)

    def waves(n, dist):
        for i in range(0, U, 16):
            for j in range(0, NR * U, 512):
                d2 = dist[i : i + 16, j : j + 512]
                inv = lax.rsqrt(d2)
                turns = d2 * inv
                f = turns - jnp.round(turns)
                u = f * f
                s = f * (WAVE[0] + u * (WAVE[1] + u * (WAVE[2] + u * WAVE[3])))
                k_ref[n, i : i + 16, j : j + 512] = ((FACTOR - s * s) * inv).astype(BF)

    def accumulate(m):
        p = jnp.concatenate([col_ref[2 * m, :E], col_ref[2 * m + 1, :E]], axis=1)
        k = jnp.concatenate([k_ref[2 * m], k_ref[2 * m + 1]], axis=0)
        acc[...] += dot(p, k)

    def saved(n):
        return pltpu.make_async_copy(k_ref.at[pl.ds(2 * n, 2)], k_hbm.at[pl.ds(2 * n, 2)], sem)

    def pair(m):
        distances(2 * m + 1, dist_b)
        waves(2 * m, dist_a)
        distances(jnp.minimum(2 * m + 2, NC - 1), dist_a)
        waves(2 * m + 1, dist_b)
        saved(m).start()

    for copy in gets:
        copy.wait()
    distances(0, dist_a)
    pair(0)

    def step(m, carry):
        accumulate(m - 1)
        pair(m)
        return carry

    lax.fori_loop(1, NC // 2, step, 0)
    accumulate(NC // 2 - 1)
    write_partials(acc, out_ref)
    pltpu.make_async_copy(k_ref, k_hbm, sem).wait()


def make_kernel(cols, rows):
    return call(
        kernel_body,
        (hbm((NC, U, NR * U), BF), hbm((NR, 3, E, U), BF)),
        flops=40 * 2 * MB,
        moved=6 * MB,
        in_specs=[IN_VMEM, IN_HBM],
        out_specs=(IN_HBM, IN_VMEM),
        scratch_shapes=[
            pltpu.VMEM((E, NR * U), F32),
            pltpu.VMEM((48, NR * U), BF),
            pltpu.VMEM((U, NR * U), F32),
            pltpu.VMEM((U, NR * U), F32),
            pltpu.VMEM((NC, U, NR * U), BF),
            pltpu.SemaphoreType.DMA,
        ],
    )(cols, *keep(rows))


def product_body(p_ref, k_ref, out_ref, acc):
    acc[...] = jnp.zeros_like(acc)
    for n in range(0, NC, 4):
        p = jnp.concatenate([p_ref[n + i] for i in range(4)], axis=1)
        k = jnp.concatenate([k_ref[n + i] for i in range(4)], axis=0)
        acc[...] += dot(p, k)
    write_partials(acc, out_ref)


def product(present, kernel):
    return call(
        product_body,
        shape((NR, 3, E, U), BF),
        flops=2 * E * 2 * MB,
        moved=5 * MB,
        in_specs=[IN_VMEM, IN_VMEM],
        out_specs=IN_VMEM,
        scratch_shapes=[pltpu.VMEM((E, NR * U), F32)],
    )(present, kernel)


def span(b):
    return ((0, 2), (1, 3)) if b == 0 else ((6, 0), (7, 1)) if b == 2 else tuple((2 + i, i) for i in range(4))


def sweep_body(last, parity, own_ref, mid, near_a, near_b, far_a, far_b, inc, mid_metas, tiles_h, prev_h, nxt_h, lefts_h, rights_h, *rest):
    if last:
        present_out, field_out = rest[:2]
    else:
        present_out, field_out = rest[0], None
    src, srcf, f1, fields, tiles, prev, nxt, lefts, rights, moves_v, moves, sems = rest[2 if last else 1 :]
    loads = [(moves_v, moves), (tiles_h, tiles)]
    loads += [(h.at[pl.ds(0, 4 * ROWS)], v) for h, v in ((prev_h, prev), (nxt_h, nxt))]
    loads += [(lefts_h, lefts), (rights_h, rights)]
    odd = parity[0]
    partners = ((6 - 6 * odd, 2 * odd, 6 - 5 * odd, 3 * odd), (6 * odd, 2 - 2 * odd, 1 + 5 * odd, 3 - 3 * odd))
    loads = [pltpu.make_async_copy(a, b, sems.at[n]) for n, (a, b) in enumerate(loads)]
    for copy in loads[1:]:
        copy.start()

    def meta(br, bc):
        if bc == 1:
            return mid_metas[16 * br : 16 * br + 16].astype(F32)
        return (far_a, far_b)[bc // 2][TAIL + 16 * br : TAIL + 16 * br + 16].astype(F32)

    moves_v[...] = jnp.zeros_like(moves_v)
    for br in range(3):
        for bc in range(3):
            o = meta(br, bc)[2:3]
            o = o + 5.0 * (jnp.where(o >= 3.0, 1.0, 0.0) + jnp.where(o >= 6.0, 1.0, 0.0))
            moves_v[3 * br + bc : 3 * br + bc + 1] = o.astype(jnp.int32)
    loads[0].start()
    line = lax.broadcasted_iota(jnp.int32, (S, U), 0).astype(F32)

    def coupling(br, bc):
        m = meta(br, bc)
        return m[0:1], jnp.where(m[1:2] == line, 1.0, 0.0).astype(BF)

    def masked(c, hi, ids):
        ids = [t.astype(F32) if isinstance(t, jax.Array) else float(t) for t in ids]
        return jnp.concatenate([c * jnp.where(hi == t, 1.0, 0.0).astype(BF) for t in ids], axis=0)

    def place(br, bc):
        hi, lo = coupling(br, bc)
        c = (near_a, mid, near_b)[bc][br * E : br * E + E]
        C, j = (2, 0) if bc == 1 else partners[bc // 2][:2]
        places = [(R * 8 + C + n, i * 4 + j + n) for R, i in span(br) for n in range(4 if bc == 1 else 2)]
        out = dot(masked(c, hi, [t for _, t in places]), lo, NT).astype(BF)
        for n, (w, _) in enumerate(places):
            src[w] = out[n * E : n * E + E]

    hi, lo = coupling(1, 1)
    own = own_ref[...]
    top = own.astype(BF)
    low = (own - top.astype(F32)).astype(BF)
    both = jnp.concatenate([masked(top, hi, range(16)), masked(low, hi, range(16))], axis=1)
    twice = jnp.concatenate([lo, lo], axis=1)
    out = dot(both, twice, NT)
    for t in range(16):
        srcf[t] = out[t * E : t * E + E]
        src[(2 + t // 4) * 8 + 2 + t % 4] = out[t * E : t * E + E].astype(BF)
    for br in range(3):
        for bc in range(3):
            if br != 1 or bc != 1:
                place(br, bc)
    for copy in loads[:2]:
        copy.wait()

    def apply(values, base, block, tile, ref, start):
        total = None
        for h in range(2):
            ks = (2 * h, 2 * h + 1)
            x = jnp.concatenate([values[base + moves[block, tile * 4 + k]] for k in ks], axis=1)
            a = [ref[start + k * S : start + k * S + S, :] for k in ks]
            y = dot(x, jnp.concatenate(a, axis=1), NT)
            total = y if total is None else total + y
        return total

    def own_tile(t, carry):
        i, j = t // 4, t % 4
        w = (2 + i) * 8 + 2 + j
        f1[w] = (srcf[t] + apply(src, w - 9, 4, t, tiles, t * ROWS)).astype(BF)
        return carry

    for t in range(16):
        own_tile(t, 0)
    for copy in loads[2:]:
        copy.wait()

    def halo(w, block, tile, ref, start):
        y = apply(src, w - 9, block, tile, ref, start)
        f1[w] = (src[w].astype(F32) + y).astype(BF)

    def edge_row(j, carry):
        halo(8 + 2 + j, 1, 12 + j, prev, j * 4 * S)
        halo(48 + 2 + j, 7, j, nxt, j * 4 * S)
        return carry

    for j in range(4):
        edge_row(j, 0)

    def edge_col(i, carry):
        w = (2 + i) * 8
        halo(w + 1, 5 - 2 * odd, i * 4 + 3, lefts, i * ROWS)
        halo(w + 6, 3 + 2 * odd, i * 4, rights, i * ROWS)
        return carry

    for i in range(4):
        edge_col(i, 0)
    for n, ref in enumerate((far_a, far_b)):
        halo(8 + partners[n][2], 2 * n, 12 + partners[n][3], ref, HEAD)
        halo(48 + partners[n][2], 6 + 2 * n, partners[n][3], ref, HEAD + ROWS)

    def final_tile(t, carry):
        i, j = t // 4, t % 4
        w = (2 + i) * 8 + 2 + j
        field = srcf[t] + apply(f1, w - 9, 4, t, tiles, t * ROWS)
        if last:
            field_out[pl.ds(t, E, stride=16), :] = field
        a = field.astype(BF)
        fields[t, :, :S] = a
        fields[t, :, S:] = (field - a.astype(F32)).astype(BF)
        return carry

    for t in range(16):
        final_tile(t, 0)
    y = dot(fields[...].reshape(16 * E, 2 * S), jnp.concatenate([lo, lo], axis=0))
    read = jnp.zeros((E, U), F32)
    for t in range(16):
        read += jnp.where(hi == float(t), y[t * E : t * E + E], 0.0)
    present = (inc[...].astype(F32) + read).astype(BF)
    if last:
        present_out[...] = present
    else:
        for c in range(NC):
            present_out[c] = present


def sweep(last, *args):
    if last:
        out = (shape((E, U), BF), shape((E * 16, S), F32))
    else:
        out = shape((NC, E, U), BF)

    def body(*refs):
        sweep_body(last, *refs)

    return call(
        body,
        out,
        flops=2 * E * S * S * 4 * 52,
        moved=6 * MB,
        in_specs=[IN_SMEM] + [IN_VMEM] * 8 + [IN_HBM] * 5,
        out_specs=(IN_VMEM, IN_VMEM) if last else IN_VMEM,
        scratch_shapes=[
            pltpu.VMEM((64, E, S), BF),
            pltpu.VMEM((16, E, S), F32),
            pltpu.VMEM((64, E, S), BF),
            pltpu.VMEM((16, E, 2 * S), BF),
            pltpu.VMEM((16 * ROWS, S), BF),
            pltpu.VMEM((4 * ROWS, S), BF),
            pltpu.VMEM((4 * ROWS, S), BF),
            pltpu.VMEM((4 * ROWS, S), BF),
            pltpu.VMEM((4 * ROWS, S), BF),
            pltpu.VMEM((16, U), jnp.int32),
            pltpu.SMEM((16, U), jnp.int32),
            pltpu.SemaphoreType.DMA((6,)),
        ],
    )(*args[:9], *keep(*args[9:]))


def shift(axis):
    size = lax.axis_size(axis)
    up = [(i, i + 1) for i in range(size - 1)]
    return up, [(j, i) for i, j in up]


def per_device(traces, incident, points, coupling, volume_tiles, tile_columns):
    row_up, row_down = shift("row")
    col_up, col_down = shift("col")
    parity = (lax.axis_index("col") % 2).reshape(1)
    swap_a = [(c, c ^ 1) for c in range(NC)]
    swap_b = [(c, ((c - 1) ^ 1) + 1) for c in range(1, NC - 1)]
    tiles = volume_tiles.reshape(16 * ROWS, S)
    rows, cols, up, down, meta = pack(traces, points, coupling.reshape(1, U), tile_columns, tiles)
    rows = lax.all_to_all(rows, "row", 0, 0, tiled=True)
    cols = lax.all_to_all(cols, "col", 0, 0, tiled=True)
    lefts, rights = fill(tiles)
    lefts = lax.ppermute(lefts, "col", col_up)
    rights = lax.ppermute(rights, "col", col_down)
    prev = lax.ppermute(up, "row", row_up)
    nxt = lax.ppermute(down, "row", row_down)
    kernel, partials = make_kernel(cols, rows)
    got = lax.all_to_all(partials, "row", 0, 0, tiled=True)
    own, mid, near_a, near_b, metas = near(parity, got, prev, nxt, meta)
    near_a = lax.ppermute(near_a, "col", swap_a)
    near_b = lax.ppermute(near_b, "col", swap_b)
    far = (near_a, near_b)
    for outer in range(2):
        last = outer == 1
        out = sweep(last, parity, own, mid, near_a, near_b, *far, incident, metas, tiles, prev, nxt, lefts, rights)
        if not last:
            out = lax.all_to_all(out, "col", 0, 0, tiled=True)
            partials = product(out, kernel)
            got = lax.all_to_all(partials, "row", 0, 0, tiled=True)
            sums = jnp.sum(got.astype(F32), axis=0)
            own, mid = sums[1], sums.astype(BF).reshape(HEAD, U)
            near_a = lax.ppermute(mid, "col", swap_a)
            near_b = lax.ppermute(mid, "col", swap_b)
    present, field = out
    return present, field.reshape(E, 4, 4, S)


def solution(mesh):
    in_specs = (
        P(None, ("row", "col")),
        P(None, ("row", "col")),
        P(None, ("row", "col")),
        P(("row", "col")),
        P("row", "col", None, None, None),
        P("row", "col", None),
    )
    out_specs = (P(None, ("row", "col")), P(None, "row", "col", None))
    return jax.shard_map(per_device, mesh=mesh, in_specs=in_specs, out_specs=out_specs, check_vma=False)
```

```python
import math

import jax
import jax.numpy as jnp
from jax import lax
from jax.experimental import pallas as pl
from jax.experimental.pallas import tpu as pltpu
from jax.sharding import PartitionSpec as P


E, U, S = 64, 128, 128
NR, NC = 8, 16
TOTAL = U * NR * NC
MB = 1 << 20
HEAD = 3 * E
ROWS = 4 * S
TAIL = 2 * ROWS
BF, F32 = jnp.bfloat16, jnp.float32
SIN = (3.14158202, -5.1671428, 2.54189903, -0.55463619)
NT = (((1,), (1,)), ((), ()))
TN = (((0,), (0,)), ((), ()))

SPACING = float(TOTAL) ** (-1.0 / 3.0)
TURNS = 2.0 / SPACING / (2.0 * math.pi)
SMOOTH = (0.5 * SPACING) ** 2 * TURNS * TURNS
FACTOR = TURNS / math.sqrt(2.0 * TOTAL)
WAVE = tuple(c * math.sqrt(2.0 * FACTOR) for c in SIN)


def dot(a, b, dims=(((1,), (0,)), ((), ()))):
    return lax.dot_general(a, b, dims, preferred_element_type=F32)


def call(body, out_shape, *, limit=24 * MB, flops=0, moved=0, **kwargs):
    return pl.pallas_call(
        body,
        out_shape=out_shape,
        compiler_params=pltpu.CompilerParams(vmem_limit_bytes=limit),
        cost_estimate=pl.CostEstimate(flops=flops, bytes_accessed=moved, transcendentals=0),
        **kwargs,
    )


def shape(dims, dtype):
    return jax.ShapeDtypeStruct(dims, dtype)


def hbm(dims, dtype):
    return pltpu.MemorySpace.HBM(dims, dtype)


def vmem(dims, dtype):
    return pltpu.MemorySpace.VMEM(dims, dtype)


def keep(*values):
    return tuple(pltpu.with_memory_space_constraint(v, pltpu.MemorySpace.HBM) for v in values)


IN_VMEM = pl.BlockSpec(memory_space=pltpu.VMEM)
IN_SMEM = pl.BlockSpec(memory_space=pltpu.SMEM)
IN_HBM = pl.BlockSpec(memory_space=pltpu.HBM)
IN_ANY = pl.BlockSpec(memory_space=pl.ANY)


def split3(x):
    a = x.astype(BF).astype(F32)
    b = (x - a).astype(BF).astype(F32)
    return a, b, (x - a - b).astype(BF).astype(F32)


def rows_at(line, pieces):
    out = jnp.zeros((16, U), F32)
    for at, value in pieces:
        out = jnp.where(line == at, value, out)
    return out


def pack_body(traces_h, points_h, coupling_h, columns_h, tiles, row_out, col_out, up, down, meta_out, *scratch):
    traces, points, coupling, columns, sems = scratch
    loads = [(points_h, points), (columns_h, columns), (coupling_h, coupling), (traces_h, traces)]
    loads += [(tiles.at[pl.ds(12 * ROWS, 4 * ROWS)], up.at[pl.ds(0, 4 * ROWS)])]
    loads += [(tiles.at[pl.ds(0, 4 * ROWS)], down.at[pl.ds(0, 4 * ROWS)])]
    loads = [pltpu.make_async_copy(a, b, sems.at[n]) for n, (a, b) in enumerate(loads)]
    for copy in loads:
        copy.start()
    lane = lax.broadcasted_iota(jnp.int32, (1, U), 1)
    loads[0].wait()
    p = (points[...] - 0.5) * TURNS
    parts = split3(p)
    norm = jnp.sum(p * p, axis=0, keepdims=True)
    line = lax.broadcasted_iota(jnp.int32, (16, U), 0)
    source = [(3 * i + d, parts[i][d : d + 1]) for i in range(3) for d in range(3)]
    source += [(9 + i, v) for i, v in enumerate(split3(norm))] + [(12, 1.0)]
    source = rows_at(line, source).astype(BF)
    shifted = split3(norm + SMOOTH)
    target = []
    for j in range(3):
        pieces = [(3 * i + d, -2.0 * parts[j][d : d + 1]) for i in range(3) for d in range(3)]
        if j == 0:
            pieces += [(9 + i, 1.0) for i in range(3)]
        target.append(rows_at(line, pieces + [(12, shifted[j])]).astype(BF))
    for r in range(NR):
        for j in range(3):
            row_out[r, 16 * j : 16 * j + 16] = target[j]
    loads[1].wait()
    offsets = jnp.zeros((1, U), jnp.int32)
    for n in range(64):
        offsets = jnp.where(lane == n, columns[n // 16, n // 4 % 4, n % 4], offsets)
    loads[2].wait()
    at = coupling[...]
    meta = [(0, (at >> 7).astype(F32)), (1, (at & 127).astype(F32)), (2, offsets.astype(F32))]
    meta = rows_at(line, meta).astype(BF)
    meta_out[...] = meta
    up[4 * ROWS :] = meta
    down[4 * ROWS :] = meta
    loads[3].wait()
    for c in range(NC):
        col_out[c, :E] = traces[...]
        col_out[c, E:] = source
    for copy in loads[4:]:
        copy.wait()


def pack(traces, points, coupling, columns, tiles):
    side = hbm((4 * ROWS + 16, S), BF)
    return call(
        pack_body,
        (hbm((NR, 48, U), BF), hbm((NC, E + 16, U), BF), side, side, vmem((16, U), BF)),
        in_specs=[IN_HBM] * 5,
        out_specs=(IN_VMEM,) * 5,
        scratch_shapes=[
            pltpu.VMEM((E, U), BF),
            pltpu.VMEM((3, U), F32),
            pltpu.VMEM((1, U), jnp.int32),
            pltpu.SMEM((4, 4, 4), jnp.int32),
            pltpu.SemaphoreType.DMA((6,)),
        ],
    )(*keep(traces, points, coupling, columns, tiles))


def column_of(odd, side):
    return 3 * odd if side else 3 - 3 * odd


def fill_body(tiles, left_out, right_out, sems):
    copies = []
    for out, j in ((left_out, 3), (right_out, 0)):
        for i in range(4):
            piece = tiles.at[pl.ds((4 * i + j) * ROWS, ROWS)]
            copies.append(pltpu.make_async_copy(piece, out.at[pl.ds(i * ROWS, ROWS)], sems.at[len(copies)]))
    for copy in copies:
        copy.start()
    for copy in copies:
        copy.wait()


def fill(tiles):
    side = shape((4 * ROWS, S), BF)
    return call(
        fill_body,
        (side, side),
        moved=2 * MB,
        in_specs=[IN_HBM],
        out_specs=(IN_VMEM,) * 2,
        scratch_shapes=[pltpu.SemaphoreType.DMA((8,))],
    )(*keep(tiles))


def corner_body(parity, prev, nxt, meta, out_a, out_b, meta_out, sems):
    copies = []
    for side, out in enumerate((out_a, out_b)):
        j = column_of(parity[0], side)
        for n, source in enumerate((prev, nxt)):
            piece = source.at[pl.ds(pl.multiple_of(j * ROWS, ROWS), ROWS)]
            copies.append(pltpu.make_async_copy(piece, out.at[pl.ds(n * ROWS, ROWS)], sems.at[len(copies)]))
    for n, source in enumerate((prev, nxt)):
        piece = source.at[pl.ds(4 * ROWS, 16)]
        copies.append(pltpu.make_async_copy(piece, meta_out.at[pl.ds(32 * n, 16)], sems.at[len(copies)]))
    for copy in copies:
        copy.start()
    meta_out[16:32] = meta[...]
    for copy in copies[4:]:
        copy.wait()
    metas = meta_out[...]
    out_a[TAIL:] = metas
    out_b[TAIL:] = metas
    for copy in copies[:4]:
        copy.wait()


def corners(parity, prev, nxt, meta):
    side = shape((TAIL + 48, S), BF)
    return call(
        corner_body,
        (side, side, shape((48, U), BF)),
        moved=2 * MB,
        in_specs=[IN_SMEM, IN_ANY, IN_ANY, IN_VMEM],
        out_specs=(IN_VMEM,) * 3,
        scratch_shapes=[pltpu.SemaphoreType.DMA((6,))],
    )(parity, prev, nxt, meta)


def near_body(got, own_out, mid_out):
    for j in range(3):
        total = got[0, j].astype(F32)
        for r in range(1, NR):
            total += got[r, j].astype(F32)
        if j == 1:
            own_out[...] = total
        mid_out[j * E : j * E + E] = total.astype(BF)


def near(got):
    return call(
        near_body,
        (shape((E, U), F32), shape((HEAD, U), BF)),
        in_specs=[IN_VMEM],
        out_specs=(IN_VMEM,) * 2,
    )(got)


def write_partials(acc, out):
    for d in range(NR):
        for j in range(3):
            b = d - 1 + j
            if 0 <= b < NR:
                out[d, j] = acc[:, b * U : b * U + U].astype(BF)
            else:
                out[d, j] = jnp.zeros((E, U), BF)


def kernel_body(col_ref, row_ref, k_hbm, out_ref, acc, feats, dist_a, dist_b, k_ref, sem):
    gets = [pltpu.make_async_copy(row_ref.at[r], feats.at[:, pl.ds(r * U, U)], sem) for r in range(NR)]
    for copy in gets:
        copy.start()
    acc[...] = jnp.zeros_like(acc)

    def distances(n, out):
        own = col_ref[n, E:]
        out[...] = dot(jnp.concatenate([own, own, own], axis=0), feats[...], TN)

    def waves(n, dist):
        for i in range(0, U, 16):
            for j in range(0, NR * U, 512):
                d2 = dist[i : i + 16, j : j + 512]
                inv = lax.rsqrt(d2)
                turns = d2 * inv
                f = turns - jnp.round(turns)
                u = f * f
                s = f * (WAVE[0] + u * (WAVE[1] + u * (WAVE[2] + u * WAVE[3])))
                k_ref[n, i : i + 16, j : j + 512] = ((FACTOR - s * s) * inv).astype(BF)

    def accumulate(m):
        p = jnp.concatenate([col_ref[2 * m, :E], col_ref[2 * m + 1, :E]], axis=1)
        k = jnp.concatenate([k_ref[2 * m], k_ref[2 * m + 1]], axis=0)
        acc[...] += dot(p, k)

    def saved(n):
        return pltpu.make_async_copy(k_ref.at[pl.ds(2 * n, 2)], k_hbm.at[pl.ds(2 * n, 2)], sem)

    def pair(m):
        distances(2 * m + 1, dist_b)
        waves(2 * m, dist_a)
        distances(jnp.minimum(2 * m + 2, NC - 1), dist_a)
        waves(2 * m + 1, dist_b)
        saved(m).start()

    for copy in gets:
        copy.wait()
    distances(0, dist_a)
    pair(0)

    def step(m, carry):
        accumulate(m - 1)
        pair(m)
        return carry

    lax.fori_loop(1, NC // 2, step, 0)
    accumulate(NC // 2 - 1)
    write_partials(acc, out_ref)
    pltpu.make_async_copy(k_ref, k_hbm, sem).wait()


def make_kernel(cols, rows):
    return call(
        kernel_body,
        (hbm((NC, U, NR * U), BF), hbm((NR, 3, E, U), BF)),
        flops=40 * 2 * MB,
        moved=6 * MB,
        in_specs=[IN_VMEM, IN_HBM],
        out_specs=(IN_HBM, IN_VMEM),
        scratch_shapes=[
            pltpu.VMEM((E, NR * U), F32),
            pltpu.VMEM((48, NR * U), BF),
            pltpu.VMEM((U, NR * U), F32),
            pltpu.VMEM((U, NR * U), F32),
            pltpu.VMEM((NC, U, NR * U), BF),
            pltpu.SemaphoreType.DMA,
        ],
    )(cols, *keep(rows))


def product_body(p_ref, k_ref, out_ref, acc):
    acc[...] = jnp.zeros_like(acc)
    for n in range(0, NC, 4):
        p = jnp.concatenate([p_ref[n + i] for i in range(4)], axis=1)
        k = jnp.concatenate([k_ref[n + i] for i in range(4)], axis=0)
        acc[...] += dot(p, k)
    write_partials(acc, out_ref)


def product(present, kernel):
    return call(
        product_body,
        shape((NR, 3, E, U), BF),
        flops=2 * E * 2 * MB,
        moved=5 * MB,
        in_specs=[IN_VMEM, IN_VMEM],
        out_specs=IN_VMEM,
        scratch_shapes=[pltpu.VMEM((E, NR * U), F32)],
    )(present, kernel)


def span(b):
    return ((0, 2), (1, 3)) if b == 0 else ((6, 0), (7, 1)) if b == 2 else tuple((2 + i, i) for i in range(4))


def sweep_body(last, parity, own_ref, mid, near_a, near_b, far_a, far_b, inc, mid_metas, tiles_h, prev_h, nxt_h, lefts_h, rights_h, *rest):
    if last:
        present_out, field_out = rest[:2]
    else:
        present_out, field_out = rest[0], None
    src, srcf, f1, fields, tiles, prev, nxt, lefts, rights, moves_v, moves, sems = rest[2 if last else 1 :]
    loads = [(moves_v, moves), (tiles_h, tiles)]
    loads += [(h.at[pl.ds(0, 4 * ROWS)], v) for h, v in ((prev_h, prev), (nxt_h, nxt))]
    loads += [(lefts_h, lefts), (rights_h, rights)]
    odd = parity[0]
    partners = ((6 - 6 * odd, 2 * odd, 6 - 5 * odd, 3 * odd), (6 * odd, 2 - 2 * odd, 1 + 5 * odd, 3 - 3 * odd))
    loads = [pltpu.make_async_copy(a, b, sems.at[n]) for n, (a, b) in enumerate(loads)]
    for copy in loads[1:]:
        copy.start()

    def meta(br, bc):
        if bc == 1:
            return mid_metas[16 * br : 16 * br + 16].astype(F32)
        return (far_a, far_b)[bc // 2][TAIL + 16 * br : TAIL + 16 * br + 16].astype(F32)

    moves_v[...] = jnp.zeros_like(moves_v)
    for br in range(3):
        for bc in range(3):
            o = meta(br, bc)[2:3]
            o = o + 5.0 * (jnp.where(o >= 3.0, 1.0, 0.0) + jnp.where(o >= 6.0, 1.0, 0.0))
            moves_v[3 * br + bc : 3 * br + bc + 1] = o.astype(jnp.int32)
    loads[0].start()
    line = lax.broadcasted_iota(jnp.int32, (S, U), 0).astype(F32)

    def coupling(br, bc):
        m = meta(br, bc)
        return m[0:1], jnp.where(m[1:2] == line, 1.0, 0.0).astype(BF)

    def masked(c, hi, ids):
        ids = [t.astype(F32) if isinstance(t, jax.Array) else float(t) for t in ids]
        return jnp.concatenate([c * jnp.where(hi == t, 1.0, 0.0).astype(BF) for t in ids], axis=0)

    def place(br, bc):
        hi, lo = coupling(br, bc)
        c = (near_a, mid, near_b)[bc][br * E : br * E + E]
        C, j = (2, 0) if bc == 1 else partners[bc // 2][:2]
        places = [(R * 8 + C + n, i * 4 + j + n) for R, i in span(br) for n in range(4 if bc == 1 else 2)]
        out = dot(masked(c, hi, [t for _, t in places]), lo, NT).astype(BF)
        for n, (w, _) in enumerate(places):
            src[w] = out[n * E : n * E + E]

    hi, lo = coupling(1, 1)
    own = own_ref[...]
    top = own.astype(BF)
    low = (own - top.astype(F32)).astype(BF)
    both = jnp.concatenate([masked(top, hi, range(16)), masked(low, hi, range(16))], axis=1)
    twice = jnp.concatenate([lo, lo], axis=1)
    out = dot(both, twice, NT)
    for t in range(16):
        srcf[t] = out[t * E : t * E + E]
        src[(2 + t // 4) * 8 + 2 + t % 4] = out[t * E : t * E + E].astype(BF)
    for br in range(3):
        for bc in range(3):
            if br != 1 or bc != 1:
                place(br, bc)
    for copy in loads[:2]:
        copy.wait()

    def apply(values, base, block, tile, ref, start):
        total = None
        for h in range(2):
            ks = (2 * h, 2 * h + 1)
            x = jnp.concatenate([values[base + moves[block, tile * 4 + k]] for k in ks], axis=1)
            a = [ref[start + k * S : start + k * S + S, :] for k in ks]
            y = dot(x, jnp.concatenate(a, axis=1), NT)
            total = y if total is None else total + y
        return total

    def own_tile(t, carry):
        i, j = t // 4, t % 4
        w = (2 + i) * 8 + 2 + j
        f1[w] = (srcf[t] + apply(src, w - 9, 4, t, tiles, t * ROWS)).astype(BF)
        return carry

    for t in range(16):
        own_tile(t, 0)
    for copy in loads[2:]:
        copy.wait()

    def halo(w, block, tile, ref, start):
        y = apply(src, w - 9, block, tile, ref, start)
        f1[w] = (src[w].astype(F32) + y).astype(BF)

    def edge_row(j, carry):
        halo(8 + 2 + j, 1, 12 + j, prev, j * 4 * S)
        halo(48 + 2 + j, 7, j, nxt, j * 4 * S)
        return carry

    for j in range(4):
        edge_row(j, 0)

    def edge_col(i, carry):
        w = (2 + i) * 8
        halo(w + 1, 5 - 2 * odd, i * 4 + 3, lefts, i * ROWS)
        halo(w + 6, 3 + 2 * odd, i * 4, rights, i * ROWS)
        return carry

    for i in range(4):
        edge_col(i, 0)
    for n, ref in enumerate((far_a, far_b)):
        halo(8 + partners[n][2], 2 * n, 12 + partners[n][3], ref, 0)
        halo(48 + partners[n][2], 6 + 2 * n, partners[n][3], ref, ROWS)

    def final_tile(t, carry):
        i, j = t // 4, t % 4
        w = (2 + i) * 8 + 2 + j
        field = srcf[t] + apply(f1, w - 9, 4, t, tiles, t * ROWS)
        if last:
            field_out[pl.ds(t, E, stride=16), :] = field
        a = field.astype(BF)
        fields[t, :, :S] = a
        fields[t, :, S:] = (field - a.astype(F32)).astype(BF)
        return carry

    for t in range(16):
        final_tile(t, 0)
    y = dot(fields[...].reshape(16 * E, 2 * S), jnp.concatenate([lo, lo], axis=0))
    read = jnp.zeros((E, U), F32)
    for t in range(16):
        read += jnp.where(hi == float(t), y[t * E : t * E + E], 0.0)
    present = (inc[...].astype(F32) + read).astype(BF)
    if last:
        present_out[...] = present
    else:
        for c in range(NC):
            present_out[c] = present


def sweep(last, *args):
    if last:
        out = (shape((E, U), BF), shape((E * 16, S), F32))
    else:
        out = shape((NC, E, U), BF)

    def body(*refs):
        sweep_body(last, *refs)

    return call(
        body,
        out,
        flops=2 * E * S * S * 4 * 52,
        moved=6 * MB,
        in_specs=[IN_SMEM] + [IN_VMEM] * 8 + [IN_HBM] * 5,
        out_specs=(IN_VMEM, IN_VMEM) if last else IN_VMEM,
        scratch_shapes=[
            pltpu.VMEM((64, E, S), BF),
            pltpu.VMEM((16, E, S), F32),
            pltpu.VMEM((64, E, S), BF),
            pltpu.VMEM((16, E, 2 * S), BF),
            pltpu.VMEM((16 * ROWS, S), BF),
            pltpu.VMEM((4 * ROWS, S), BF),
            pltpu.VMEM((4 * ROWS, S), BF),
            pltpu.VMEM((4 * ROWS, S), BF),
            pltpu.VMEM((4 * ROWS, S), BF),
            pltpu.VMEM((16, U), jnp.int32),
            pltpu.SMEM((16, U), jnp.int32),
            pltpu.SemaphoreType.DMA((6,)),
        ],
    )(*args[:9], *keep(*args[9:]))


def shift(axis):
    size = lax.axis_size(axis)
    up = [(i, i + 1) for i in range(size - 1)]
    return up, [(j, i) for i, j in up]


def per_device(traces, incident, points, coupling, volume_tiles, tile_columns):
    row_up, row_down = shift("row")
    col_up, col_down = shift("col")
    parity = (lax.axis_index("col") % 2).reshape(1)
    swap_a = [(c, c ^ 1) for c in range(NC)]
    swap_b = [(c, ((c - 1) ^ 1) + 1) for c in range(1, NC - 1)]
    tiles = volume_tiles.reshape(16 * ROWS, S)
    rows, cols, up, down, meta = pack(traces, points, coupling.reshape(1, U), tile_columns, tiles)
    rows = lax.all_to_all(rows, "row", 0, 0, tiled=True)
    cols = lax.all_to_all(cols, "col", 0, 0, tiled=True)
    lefts, rights = fill(tiles)
    lefts = lax.ppermute(lefts, "col", col_up)
    rights = lax.ppermute(rights, "col", col_down)
    prev = lax.ppermute(up, "row", row_up)
    nxt = lax.ppermute(down, "row", row_down)
    kernel, partials = make_kernel(cols, rows)
    got = lax.all_to_all(partials, "row", 0, 0, tiled=True)
    far_a, far_b, metas = corners(parity, prev, nxt, meta)
    far_a = lax.ppermute(far_a, "col", swap_a)
    far_b = lax.ppermute(far_b, "col", swap_b)
    for outer in range(2):
        last = outer == 1
        own, mid = near(got)
        near_a = lax.ppermute(mid, "col", swap_a)
        near_b = lax.ppermute(mid, "col", swap_b)
        out = sweep(
            last, parity, own, mid, near_a, near_b, far_a, far_b, incident, metas, tiles, prev, nxt, lefts, rights
        )
        if not last:
            out = lax.all_to_all(out, "col", 0, 0, tiled=True)
            partials = product(out, kernel)
            got = lax.all_to_all(partials, "row", 0, 0, tiled=True)
    present, field = out
    return present, field.reshape(E, 4, 4, S)


def solution(mesh):
    in_specs = (
        P(None, ("row", "col")),
        P(None, ("row", "col")),
        P(None, ("row", "col")),
        P(("row", "col")),
        P("row", "col", None, None, None),
        P("row", "col", None),
    )
    out_specs = (P(None, ("row", "col")), P(None, "row", "col", None))
    return jax.shard_map(per_device, mesh=mesh, in_specs=in_specs, out_specs=out_specs, check_vma=False)
```

```python
import math

import jax
import jax.numpy as jnp
from jax import lax
from jax.experimental import pallas as pl
from jax.experimental.pallas import tpu as pltpu
from jax.sharding import PartitionSpec as P


E, U, S = 64, 128, 128
NR, NC = 8, 16
TOTAL = U * NR * NC
MB = 1 << 20
HEAD = 3 * E
ROWS = 4 * S
TAIL = 2 * ROWS
BF, F32 = jnp.bfloat16, jnp.float32
SIN = (3.14158202, -5.1671428, 2.54189903, -0.55463619)
NT = (((1,), (1,)), ((), ()))
TN = (((0,), (0,)), ((), ()))

SPACING = float(TOTAL) ** (-1.0 / 3.0)
TURNS = 2.0 / SPACING / (2.0 * math.pi)
SMOOTH = (0.5 * SPACING) ** 2 * TURNS * TURNS
FACTOR = TURNS / math.sqrt(2.0 * TOTAL)
WAVE = tuple(c * math.sqrt(2.0 * FACTOR) for c in SIN)


def dot(a, b, dims=(((1,), (0,)), ((), ()))):
    return lax.dot_general(a, b, dims, preferred_element_type=F32)


def call(body, out_shape, *, limit=24 * MB, flops=0, moved=0, **kwargs):
    return pl.pallas_call(
        body,
        out_shape=out_shape,
        compiler_params=pltpu.CompilerParams(vmem_limit_bytes=limit),
        cost_estimate=pl.CostEstimate(flops=flops, bytes_accessed=moved, transcendentals=0),
        **kwargs,
    )


def shape(dims, dtype):
    return jax.ShapeDtypeStruct(dims, dtype)


def hbm(dims, dtype):
    return pltpu.MemorySpace.HBM(dims, dtype)


def keep(*values):
    return tuple(pltpu.with_memory_space_constraint(v, pltpu.MemorySpace.HBM) for v in values)


IN_VMEM = pl.BlockSpec(memory_space=pltpu.VMEM)
IN_SMEM = pl.BlockSpec(memory_space=pltpu.SMEM)
IN_HBM = pl.BlockSpec(memory_space=pltpu.HBM)
IN_ANY = pl.BlockSpec(memory_space=pl.ANY)


def split3(x):
    a = x.astype(BF).astype(F32)
    b = (x - a).astype(BF).astype(F32)
    return a, b, (x - a - b).astype(BF).astype(F32)


def rows_at(line, pieces):
    out = jnp.zeros((16, U), F32)
    for at, value in pieces:
        out = jnp.where(line == at, value, out)
    return out


def pack_body(traces_h, points_h, row_out, col_out, traces, points, sems):
    loads = [(points_h, points), (traces_h, traces)]
    loads = [pltpu.make_async_copy(a, b, sems.at[n]) for n, (a, b) in enumerate(loads)]
    for copy in loads:
        copy.start()
    loads[0].wait()
    p = (points[...] - 0.5) * TURNS
    parts = split3(p)
    norm = jnp.sum(p * p, axis=0, keepdims=True)
    line = lax.broadcasted_iota(jnp.int32, (16, U), 0)
    source = [(3 * i + d, parts[i][d : d + 1]) for i in range(3) for d in range(3)]
    source += [(9 + i, v) for i, v in enumerate(split3(norm))] + [(12, 1.0)]
    source = rows_at(line, source).astype(BF)
    shifted = split3(norm + SMOOTH)
    target = []
    for j in range(3):
        pieces = [(3 * i + d, -2.0 * parts[j][d : d + 1]) for i in range(3) for d in range(3)]
        if j == 0:
            pieces += [(9 + i, 1.0) for i in range(3)]
        target.append(rows_at(line, pieces + [(12, shifted[j])]).astype(BF))
    for r in range(NR):
        for j in range(3):
            row_out[r, 16 * j : 16 * j + 16] = target[j]
    loads[1].wait()
    for c in range(NC):
        col_out[c, :E] = traces[...]
        col_out[c, E:] = source


def pack(traces, points):
    return call(
        pack_body,
        (hbm((NR, 48, U), BF), hbm((NC, E + 16, U), BF)),
        in_specs=[IN_HBM] * 2,
        out_specs=(IN_VMEM,) * 2,
        scratch_shapes=[pltpu.VMEM((E, U), BF), pltpu.VMEM((3, U), F32), pltpu.SemaphoreType.DMA((2,))],
    )(*keep(traces, points))


def slices_body(coupling_h, columns_h, tiles, up, down, meta_out, coupling, columns, sems):
    loads = [(columns_h, columns), (coupling_h, coupling)]
    loads += [(tiles.at[pl.ds(12 * ROWS, 4 * ROWS)], up.at[pl.ds(0, 4 * ROWS)])]
    loads += [(tiles.at[pl.ds(0, 4 * ROWS)], down.at[pl.ds(0, 4 * ROWS)])]
    loads = [pltpu.make_async_copy(a, b, sems.at[n]) for n, (a, b) in enumerate(loads)]
    for copy in loads:
        copy.start()
    lane = lax.broadcasted_iota(jnp.int32, (1, U), 1)
    line = lax.broadcasted_iota(jnp.int32, (16, U), 0)
    loads[0].wait()
    offsets = jnp.zeros((1, U), jnp.int32)
    for n in range(64):
        offsets = jnp.where(lane == n, columns[n // 16, n // 4 % 4, n % 4], offsets)
    loads[1].wait()
    at = coupling[...]
    meta = [(0, (at >> 7).astype(F32)), (1, (at & 127).astype(F32)), (2, offsets.astype(F32))]
    meta = rows_at(line, meta).astype(BF)
    meta_out[...] = meta
    up[4 * ROWS :] = meta
    down[4 * ROWS :] = meta
    for copy in loads[2:]:
        copy.wait()


def slices(coupling, columns, tiles):
    side = hbm((4 * ROWS + 16, S), BF)
    return call(
        slices_body,
        (side, side, shape((16, U), BF)),
        moved=2 * MB,
        in_specs=[IN_HBM] * 3,
        out_specs=(IN_VMEM,) * 3,
        scratch_shapes=[
            pltpu.VMEM((1, U), jnp.int32),
            pltpu.SMEM((4, 4, 4), jnp.int32),
            pltpu.SemaphoreType.DMA((4,)),
        ],
    )(*keep(coupling, columns, tiles))


def column_of(odd, side):
    return 3 * odd if side else 3 - 3 * odd


def fill_body(parity, tiles, out_a, out_b, sems):
    copies = []
    for side, out in enumerate((out_a, out_b)):
        j = column_of(parity[0], side)
        for i in range(4):
            piece = tiles.at[pl.ds(pl.multiple_of((4 * i + j) * ROWS, ROWS), ROWS)]
            copies.append(pltpu.make_async_copy(piece, out.at[pl.ds(i * ROWS, ROWS)], sems.at[len(copies)]))
    for copy in copies:
        copy.start()
    for copy in copies:
        copy.wait()


def fill(parity, tiles):
    side = shape((4 * ROWS, S), BF)
    return call(
        fill_body,
        (side, side),
        moved=2 * MB,
        in_specs=[IN_SMEM, IN_HBM],
        out_specs=(IN_VMEM,) * 2,
        scratch_shapes=[pltpu.SemaphoreType.DMA((8,))],
    )(parity, *keep(tiles))


def corner_body(parity, prev, nxt, meta, out_a, out_b, meta_out, sems):
    copies = []
    for side, out in enumerate((out_a, out_b)):
        j = column_of(parity[0], side)
        for n, source in enumerate((prev, nxt)):
            piece = source.at[pl.ds(pl.multiple_of(j * ROWS, ROWS), ROWS)]
            copies.append(pltpu.make_async_copy(piece, out.at[pl.ds(n * ROWS, ROWS)], sems.at[len(copies)]))
    for n, source in enumerate((prev, nxt)):
        piece = source.at[pl.ds(4 * ROWS, 16)]
        copies.append(pltpu.make_async_copy(piece, meta_out.at[pl.ds(32 * n, 16)], sems.at[len(copies)]))
    for copy in copies:
        copy.start()
    meta_out[16:32] = meta[...]
    for copy in copies[4:]:
        copy.wait()
    metas = meta_out[...]
    out_a[TAIL:] = metas
    out_b[TAIL:] = metas
    for copy in copies[:4]:
        copy.wait()


def corners(parity, prev, nxt, meta):
    side = shape((TAIL + 48, S), BF)
    return call(
        corner_body,
        (side, side, shape((48, U), BF)),
        moved=2 * MB,
        in_specs=[IN_SMEM, IN_ANY, IN_ANY, IN_VMEM],
        out_specs=(IN_VMEM,) * 3,
        scratch_shapes=[pltpu.SemaphoreType.DMA((6,))],
    )(parity, prev, nxt, meta)


def near_body(got, own_out, mid_out):
    for j in range(3):
        total = got[0, j].astype(F32)
        for r in range(1, NR):
            total += got[r, j].astype(F32)
        if j == 1:
            own_out[...] = total
        mid_out[j * E : j * E + E] = total.astype(BF)


def near(got):
    return call(
        near_body,
        (shape((E, U), F32), shape((HEAD, U), BF)),
        in_specs=[IN_VMEM],
        out_specs=(IN_VMEM,) * 2,
    )(got)


def write_partials(acc, out):
    for d in range(NR):
        for j in range(3):
            b = d - 1 + j
            if 0 <= b < NR:
                out[d, j] = acc[:, b * U : b * U + U].astype(BF)
            else:
                out[d, j] = jnp.zeros((E, U), BF)


def kernel_body(col_ref, row_ref, k_hbm, out_ref, acc, feats, dist_a, dist_b, k_ref, sem):
    gets = [pltpu.make_async_copy(row_ref.at[r], feats.at[:, pl.ds(r * U, U)], sem) for r in range(NR)]
    for copy in gets:
        copy.start()
    acc[...] = jnp.zeros_like(acc)

    def distances(n, out):
        own = col_ref[n, E:]
        out[...] = dot(jnp.concatenate([own, own, own], axis=0), feats[...], TN)

    def waves(n, dist):
        for i in range(0, U, 16):
            for j in range(0, NR * U, 512):
                d2 = dist[i : i + 16, j : j + 512]
                inv = lax.rsqrt(d2)
                turns = d2 * inv
                f = turns - jnp.round(turns)
                u = f * f
                s = f * (WAVE[0] + u * (WAVE[1] + u * (WAVE[2] + u * WAVE[3])))
                k_ref[n, i : i + 16, j : j + 512] = ((FACTOR - s * s) * inv).astype(BF)

    def accumulate(m):
        p = jnp.concatenate([col_ref[2 * m, :E], col_ref[2 * m + 1, :E]], axis=1)
        k = jnp.concatenate([k_ref[2 * m], k_ref[2 * m + 1]], axis=0)
        acc[...] += dot(p, k)

    def saved(n):
        return pltpu.make_async_copy(k_ref.at[pl.ds(2 * n, 2)], k_hbm.at[pl.ds(2 * n, 2)], sem)

    def pair(m):
        distances(2 * m + 1, dist_b)
        waves(2 * m, dist_a)
        distances(jnp.minimum(2 * m + 2, NC - 1), dist_a)
        waves(2 * m + 1, dist_b)
        saved(m).start()

    for copy in gets:
        copy.wait()
    distances(0, dist_a)
    pair(0)

    def step(m, carry):
        accumulate(m - 1)
        pair(m)
        return carry

    lax.fori_loop(1, NC // 2, step, 0)
    accumulate(NC // 2 - 1)
    write_partials(acc, out_ref)
    pltpu.make_async_copy(k_ref, k_hbm, sem).wait()


def make_kernel(cols, rows):
    return call(
        kernel_body,
        (hbm((NC, U, NR * U), BF), hbm((NR, 3, E, U), BF)),
        flops=40 * 2 * MB,
        moved=6 * MB,
        in_specs=[IN_VMEM, IN_HBM],
        out_specs=(IN_HBM, IN_VMEM),
        scratch_shapes=[
            pltpu.VMEM((E, NR * U), F32),
            pltpu.VMEM((48, NR * U), BF),
            pltpu.VMEM((U, NR * U), F32),
            pltpu.VMEM((U, NR * U), F32),
            pltpu.VMEM((NC, U, NR * U), BF),
            pltpu.SemaphoreType.DMA,
        ],
    )(cols, *keep(rows))


def product_body(p_ref, k_ref, out_ref, acc):
    acc[...] = jnp.zeros_like(acc)
    for n in range(0, NC, 4):
        p = jnp.concatenate([p_ref[n + i] for i in range(4)], axis=1)
        k = jnp.concatenate([k_ref[n + i] for i in range(4)], axis=0)
        acc[...] += dot(p, k)
    write_partials(acc, out_ref)


def product(present, kernel):
    return call(
        product_body,
        shape((NR, 3, E, U), BF),
        flops=2 * E * 2 * MB,
        moved=5 * MB,
        in_specs=[IN_VMEM, IN_VMEM],
        out_specs=IN_VMEM,
        scratch_shapes=[pltpu.VMEM((E, NR * U), F32)],
    )(present, kernel)


def span(b):
    return ((0, 2), (1, 3)) if b == 0 else ((6, 0), (7, 1)) if b == 2 else tuple((2 + i, i) for i in range(4))


def sweep_body(last, parity, own_ref, mid, near_a, near_b, far_a, far_b, inc, mid_metas, tiles_h, prev_h, nxt_h, edge_a_h, edge_b_h, *rest):
    if last:
        present_out, field_out = rest[:2]
    else:
        present_out, field_out = rest[0], None
    src, srcf, f1, fields, tiles, prev, nxt, edge_a, edge_b, moves_v, moves, sems = rest[2 if last else 1 :]
    loads = [(moves_v, moves), (tiles_h, tiles)]
    loads += [(h.at[pl.ds(0, 4 * ROWS)], v) for h, v in ((prev_h, prev), (nxt_h, nxt))]
    loads += [(edge_a_h, edge_a), (edge_b_h, edge_b)]
    odd = parity[0]
    partners = ((6 - 6 * odd, 2 * odd, 6 - 5 * odd, 3 * odd), (6 * odd, 2 - 2 * odd, 1 + 5 * odd, 3 - 3 * odd))
    loads = [pltpu.make_async_copy(a, b, sems.at[n]) for n, (a, b) in enumerate(loads)]
    for copy in loads[1:]:
        copy.start()

    def meta(br, bc):
        if bc == 1:
            return mid_metas[16 * br : 16 * br + 16].astype(F32)
        return (far_a, far_b)[bc // 2][TAIL + 16 * br : TAIL + 16 * br + 16].astype(F32)

    moves_v[...] = jnp.zeros_like(moves_v)
    for br in range(3):
        for bc in range(3):
            o = meta(br, bc)[2:3]
            o = o + 5.0 * (jnp.where(o >= 3.0, 1.0, 0.0) + jnp.where(o >= 6.0, 1.0, 0.0))
            moves_v[3 * br + bc : 3 * br + bc + 1] = o.astype(jnp.int32)
    loads[0].start()
    line = lax.broadcasted_iota(jnp.int32, (S, U), 0).astype(F32)

    def coupling(br, bc):
        m = meta(br, bc)
        return m[0:1], jnp.where(m[1:2] == line, 1.0, 0.0).astype(BF)

    def masked(c, hi, ids):
        ids = [t.astype(F32) if isinstance(t, jax.Array) else float(t) for t in ids]
        return jnp.concatenate([c * jnp.where(hi == t, 1.0, 0.0).astype(BF) for t in ids], axis=0)

    def place(br, bc):
        hi, lo = coupling(br, bc)
        c = (near_a, mid, near_b)[bc][br * E : br * E + E]
        C, j = (2, 0) if bc == 1 else partners[bc // 2][:2]
        places = [(R * 8 + C + n, i * 4 + j + n) for R, i in span(br) for n in range(4 if bc == 1 else 2)]
        out = dot(masked(c, hi, [t for _, t in places]), lo, NT).astype(BF)
        for n, (w, _) in enumerate(places):
            src[w] = out[n * E : n * E + E]

    hi, lo = coupling(1, 1)
    own = own_ref[...]
    top = own.astype(BF)
    low = (own - top.astype(F32)).astype(BF)
    both = jnp.concatenate([masked(top, hi, range(16)), masked(low, hi, range(16))], axis=1)
    twice = jnp.concatenate([lo, lo], axis=1)
    out = dot(both, twice, NT)
    for t in range(16):
        srcf[t] = out[t * E : t * E + E]
        src[(2 + t // 4) * 8 + 2 + t % 4] = out[t * E : t * E + E].astype(BF)
    for br in range(3):
        for bc in range(3):
            if br != 1 or bc != 1:
                place(br, bc)
    for copy in loads[:2]:
        copy.wait()

    def apply(values, base, block, tile, ref, start):
        total = None
        for h in range(2):
            ks = (2 * h, 2 * h + 1)
            x = jnp.concatenate([values[base + moves[block, tile * 4 + k]] for k in ks], axis=1)
            a = [ref[start + k * S : start + k * S + S, :] for k in ks]
            y = dot(x, jnp.concatenate(a, axis=1), NT)
            total = y if total is None else total + y
        return total

    def own_tile(t, carry):
        i, j = t // 4, t % 4
        w = (2 + i) * 8 + 2 + j
        f1[w] = (srcf[t] + apply(src, w - 9, 4, t, tiles, t * ROWS)).astype(BF)
        return carry

    for t in range(16):
        own_tile(t, 0)
    for copy in loads[2:]:
        copy.wait()

    def halo(w, block, tile, ref, start):
        y = apply(src, w - 9, block, tile, ref, start)
        f1[w] = (src[w].astype(F32) + y).astype(BF)

    def edge_row(j, carry):
        halo(8 + 2 + j, 1, 12 + j, prev, j * 4 * S)
        halo(48 + 2 + j, 7, j, nxt, j * 4 * S)
        return carry

    for j in range(4):
        edge_row(j, 0)

    def edge_col(i, carry):
        w = (2 + i) * 8
        for n, ref in enumerate((edge_a, edge_b)):
            halo(w + partners[n][2], 3 + 2 * n, i * 4 + partners[n][3], ref, i * ROWS)
        return carry

    for i in range(4):
        edge_col(i, 0)
    for n, ref in enumerate((far_a, far_b)):
        halo(8 + partners[n][2], 2 * n, 12 + partners[n][3], ref, 0)
        halo(48 + partners[n][2], 6 + 2 * n, partners[n][3], ref, ROWS)

    def final_tile(t, carry):
        i, j = t // 4, t % 4
        w = (2 + i) * 8 + 2 + j
        field = srcf[t] + apply(f1, w - 9, 4, t, tiles, t * ROWS)
        if last:
            field_out[pl.ds(t, E, stride=16), :] = field
        a = field.astype(BF)
        fields[t, :, :S] = a
        fields[t, :, S:] = (field - a.astype(F32)).astype(BF)
        return carry

    for t in range(16):
        final_tile(t, 0)
    y = dot(fields[...].reshape(16 * E, 2 * S), jnp.concatenate([lo, lo], axis=0))
    read = jnp.zeros((E, U), F32)
    for t in range(16):
        read += jnp.where(hi == float(t), y[t * E : t * E + E], 0.0)
    present = (inc[...].astype(F32) + read).astype(BF)
    if last:
        present_out[...] = present
    else:
        for c in range(NC):
            present_out[c] = present


def sweep(last, *args):
    if last:
        out = (shape((E, U), BF), shape((E * 16, S), F32))
    else:
        out = shape((NC, E, U), BF)

    def body(*refs):
        sweep_body(last, *refs)

    return call(
        body,
        out,
        flops=2 * E * S * S * 4 * 52,
        moved=6 * MB,
        in_specs=[IN_SMEM] + [IN_VMEM] * 8 + [IN_HBM] * 5,
        out_specs=(IN_VMEM, IN_VMEM) if last else IN_VMEM,
        scratch_shapes=[
            pltpu.VMEM((64, E, S), BF),
            pltpu.VMEM((16, E, S), F32),
            pltpu.VMEM((64, E, S), BF),
            pltpu.VMEM((16, E, 2 * S), BF),
            pltpu.VMEM((16 * ROWS, S), BF),
            pltpu.VMEM((4 * ROWS, S), BF),
            pltpu.VMEM((4 * ROWS, S), BF),
            pltpu.VMEM((4 * ROWS, S), BF),
            pltpu.VMEM((4 * ROWS, S), BF),
            pltpu.VMEM((16, U), jnp.int32),
            pltpu.SMEM((16, U), jnp.int32),
            pltpu.SemaphoreType.DMA((6,)),
        ],
    )(*args[:9], *keep(*args[9:]))


def shift(axis):
    size = lax.axis_size(axis)
    up = [(i, i + 1) for i in range(size - 1)]
    return up, [(j, i) for i, j in up]


def per_device(traces, incident, points, coupling, volume_tiles, tile_columns):
    row_up, row_down = shift("row")
    parity = (lax.axis_index("col") % 2).reshape(1)
    swap_a = [(c, c ^ 1) for c in range(NC)]
    swap_b = [(c, ((c - 1) ^ 1) + 1) for c in range(1, NC - 1)]
    tiles = volume_tiles.reshape(16 * ROWS, S)
    rows, cols = pack(traces, points)
    rows = lax.all_to_all(rows, "row", 0, 0, tiled=True)
    cols = lax.all_to_all(cols, "col", 0, 0, tiled=True)
    edge_a, edge_b = fill(parity, tiles)
    edge_a = lax.ppermute(edge_a, "col", swap_a)
    edge_b = lax.ppermute(edge_b, "col", swap_b)
    up, down, meta = slices(coupling.reshape(1, U), tile_columns, tiles)
    prev = lax.ppermute(up, "row", row_up)
    nxt = lax.ppermute(down, "row", row_down)
    kernel, partials = make_kernel(cols, rows)
    got = lax.all_to_all(partials, "row", 0, 0, tiled=True)
    far_a, far_b, metas = corners(parity, prev, nxt, meta)
    far_a = lax.ppermute(far_a, "col", swap_a)
    far_b = lax.ppermute(far_b, "col", swap_b)
    for outer in range(2):
        last = outer == 1
        own, mid = near(got)
        near_a = lax.ppermute(mid, "col", swap_a)
        near_b = lax.ppermute(mid, "col", swap_b)
        out = sweep(
            last, parity, own, mid, near_a, near_b, far_a, far_b, incident, metas, tiles, prev, nxt, edge_a, edge_b
        )
        if not last:
            out = lax.all_to_all(out, "col", 0, 0, tiled=True)
            partials = product(out, kernel)
            got = lax.all_to_all(partials, "row", 0, 0, tiled=True)
    present, field = out
    return present, field.reshape(E, 4, 4, S)


def solution(mesh):
    in_specs = (
        P(None, ("row", "col")),
        P(None, ("row", "col")),
        P(None, ("row", "col")),
        P(("row", "col")),
        P("row", "col", None, None, None),
        P("row", "col", None),
    )
    out_specs = (P(None, ("row", "col")), P(None, "row", "col", None))
    return jax.shard_map(per_device, mesh=mesh, in_specs=in_specs, out_specs=out_specs, check_vma=False)
```

```python
import math

import jax
import jax.numpy as jnp
from jax import lax
from jax.experimental import pallas as pl
from jax.experimental.pallas import tpu as pltpu
from jax.sharding import PartitionSpec as P


E, U, S = 64, 128, 128
NR, NC = 8, 16
TOTAL = U * NR * NC
MB = 1 << 20
HEAD = 3 * E
ROWS = 4 * S
TAIL = 2 * ROWS
BF, F32 = jnp.bfloat16, jnp.float32
SIN = (3.14158202, -5.1671428, 2.54189903, -0.55463619)
NT = (((1,), (1,)), ((), ()))
TN = (((0,), (0,)), ((), ()))

SPACING = float(TOTAL) ** (-1.0 / 3.0)
TURNS = 2.0 / SPACING / (2.0 * math.pi)
SMOOTH = (0.5 * SPACING) ** 2 * TURNS * TURNS
FACTOR = TURNS / math.sqrt(2.0 * TOTAL)
WAVE = tuple(c * math.sqrt(2.0 * FACTOR) for c in SIN)


def dot(a, b, dims=(((1,), (0,)), ((), ()))):
    return lax.dot_general(a, b, dims, preferred_element_type=F32)


def call(body, out_shape, *, limit=24 * MB, flops=0, moved=0, flags=None, **kwargs):
    return pl.pallas_call(
        body,
        out_shape=out_shape,
        compiler_params=pltpu.CompilerParams(vmem_limit_bytes=limit, **({"flags": flags} if flags else {})),
        cost_estimate=pl.CostEstimate(flops=flops, bytes_accessed=moved, transcendentals=0),
        **kwargs,
    )


def shape(dims, dtype):
    return jax.ShapeDtypeStruct(dims, dtype)


def hbm(dims, dtype):
    return pltpu.MemorySpace.HBM(dims, dtype)


def keep(*values):
    return tuple(pltpu.with_memory_space_constraint(v, pltpu.MemorySpace.HBM) for v in values)


IN_VMEM = pl.BlockSpec(memory_space=pltpu.VMEM)
IN_SMEM = pl.BlockSpec(memory_space=pltpu.SMEM)
IN_HBM = pl.BlockSpec(memory_space=pltpu.HBM)
IN_ANY = pl.BlockSpec(memory_space=pl.ANY)


def split3(x):
    a = x.astype(BF).astype(F32)
    b = (x - a).astype(BF).astype(F32)
    return a, b, (x - a - b).astype(BF).astype(F32)


def rows_at(line, pieces):
    out = jnp.zeros((16, U), F32)
    for at, value in pieces:
        out = jnp.where(line == at, value, out)
    return out


def pack_body(traces_h, points_h, row_out, col_out, traces, points, sems):
    loads = [(points_h, points), (traces_h, traces)]
    loads = [pltpu.make_async_copy(a, b, sems.at[n]) for n, (a, b) in enumerate(loads)]
    for copy in loads:
        copy.start()
    loads[0].wait()
    p = (points[...] - 0.5) * TURNS
    parts = split3(p)
    norm = jnp.sum(p * p, axis=0, keepdims=True)
    line = lax.broadcasted_iota(jnp.int32, (16, U), 0)
    source = [(3 * i + d, parts[i][d : d + 1]) for i in range(3) for d in range(3)]
    source += [(9 + i, v) for i, v in enumerate(split3(norm))] + [(12, 1.0)]
    source = rows_at(line, source).astype(BF)
    shifted = split3(norm + SMOOTH)
    target = []
    for j in range(3):
        pieces = [(3 * i + d, -2.0 * parts[j][d : d + 1]) for i in range(3) for d in range(3)]
        if j == 0:
            pieces += [(9 + i, 1.0) for i in range(3)]
        target.append(rows_at(line, pieces + [(12, shifted[j])]).astype(BF))
    for r in range(NR):
        for j in range(3):
            row_out[r, 16 * j : 16 * j + 16] = target[j]
    loads[1].wait()
    for c in range(NC):
        col_out[c, :E] = traces[...]
        col_out[c, E:] = source


def pack(traces, points):
    return call(
        pack_body,
        (hbm((NR, 48, U), BF), hbm((NC, E + 16, U), BF)),
        in_specs=[IN_HBM] * 2,
        out_specs=(IN_VMEM,) * 2,
        scratch_shapes=[pltpu.VMEM((E, U), BF), pltpu.VMEM((3, U), F32), pltpu.SemaphoreType.DMA((2,))],
    )(*keep(traces, points))


def slices_body(coupling_h, columns_h, tiles, up, down, meta_out, coupling, columns, sems):
    loads = [(columns_h, columns), (coupling_h, coupling)]
    loads += [(tiles.at[pl.ds(12 * ROWS, 4 * ROWS)], up.at[pl.ds(0, 4 * ROWS)])]
    loads += [(tiles.at[pl.ds(0, 4 * ROWS)], down.at[pl.ds(0, 4 * ROWS)])]
    loads = [pltpu.make_async_copy(a, b, sems.at[n]) for n, (a, b) in enumerate(loads)]
    for copy in loads:
        copy.start()
    lane = lax.broadcasted_iota(jnp.int32, (1, U), 1)
    line = lax.broadcasted_iota(jnp.int32, (16, U), 0)
    loads[0].wait()
    offsets = jnp.zeros((1, U), jnp.int32)
    for n in range(64):
        offsets = jnp.where(lane == n, columns[n // 16, n // 4 % 4, n % 4], offsets)
    loads[1].wait()
    at = coupling[...]
    meta = [(0, (at >> 7).astype(F32)), (1, (at & 127).astype(F32)), (2, offsets.astype(F32))]
    meta = rows_at(line, meta).astype(BF)
    meta_out[...] = meta
    up[4 * ROWS :] = meta
    down[4 * ROWS :] = meta
    for copy in loads[2:]:
        copy.wait()


def slices(coupling, columns, tiles):
    side = hbm((4 * ROWS + 16, S), BF)
    return call(
        slices_body,
        (side, side, shape((16, U), BF)),
        moved=2 * MB,
        in_specs=[IN_HBM] * 3,
        out_specs=(IN_VMEM,) * 3,
        scratch_shapes=[
            pltpu.VMEM((1, U), jnp.int32),
            pltpu.SMEM((4, 4, 4), jnp.int32),
            pltpu.SemaphoreType.DMA((4,)),
        ],
    )(*keep(coupling, columns, tiles))


def column_of(odd, side):
    return 3 * odd if side else 3 - 3 * odd


def fill_body(parity, tiles, out_a, out_b, sems):
    copies = []
    for side, out in enumerate((out_a, out_b)):
        j = column_of(parity[0], side)
        for i in range(4):
            piece = tiles.at[pl.ds(pl.multiple_of((4 * i + j) * ROWS, ROWS), ROWS)]
            copies.append(pltpu.make_async_copy(piece, out.at[pl.ds(i * ROWS, ROWS)], sems.at[len(copies)]))
    for copy in copies:
        copy.start()
    for copy in copies:
        copy.wait()


def fill(parity, tiles):
    side = shape((4 * ROWS, S), BF)
    return call(
        fill_body,
        (side, side),
        moved=2 * MB,
        in_specs=[IN_SMEM, IN_HBM],
        out_specs=(IN_VMEM,) * 2,
        scratch_shapes=[pltpu.SemaphoreType.DMA((8,))],
    )(parity, *keep(tiles))


def corner_body(parity, prev, nxt, meta, out_a, out_b, meta_out, sems):
    copies = []
    for side, out in enumerate((out_a, out_b)):
        j = column_of(parity[0], side)
        for n, source in enumerate((prev, nxt)):
            piece = source.at[pl.ds(pl.multiple_of(j * ROWS, ROWS), ROWS)]
            copies.append(pltpu.make_async_copy(piece, out.at[pl.ds(n * ROWS, ROWS)], sems.at[len(copies)]))
    for n, source in enumerate((prev, nxt)):
        piece = source.at[pl.ds(4 * ROWS, 16)]
        copies.append(pltpu.make_async_copy(piece, meta_out.at[pl.ds(32 * n, 16)], sems.at[len(copies)]))
    for copy in copies:
        copy.start()
    meta_out[16:32] = meta[...]
    for copy in copies[4:]:
        copy.wait()
    metas = meta_out[...]
    out_a[TAIL:] = metas
    out_b[TAIL:] = metas
    for copy in copies[:4]:
        copy.wait()


def corners(parity, prev, nxt, meta):
    side = shape((TAIL + 48, S), BF)
    return call(
        corner_body,
        (side, side, shape((48, U), BF)),
        moved=2 * MB,
        in_specs=[IN_SMEM, IN_ANY, IN_ANY, IN_VMEM],
        out_specs=(IN_VMEM,) * 3,
        scratch_shapes=[pltpu.SemaphoreType.DMA((6,))],
    )(parity, prev, nxt, meta)


def near_body(got, own_out, mid_out):
    for j in range(3):
        total = got[0, j].astype(F32)
        for r in range(1, NR):
            total += got[r, j].astype(F32)
        if j == 1:
            own_out[...] = total
        mid_out[j * E : j * E + E] = total.astype(BF)


def near(got):
    return call(
        near_body,
        (shape((E, U), F32), shape((HEAD, U), BF)),
        in_specs=[IN_VMEM],
        out_specs=(IN_VMEM,) * 2,
    )(got)


def write_partials(acc, out):
    for d in range(NR):
        for j in range(3):
            b = d - 1 + j
            if 0 <= b < NR:
                out[d, j] = acc[:, b * U : b * U + U].astype(BF)
            else:
                out[d, j] = jnp.zeros((E, U), BF)


def kernel_body(col_ref, row_ref, k_hbm, out_ref, acc, feats, dist_a, dist_b, k_ref, sem):
    gets = [pltpu.make_async_copy(row_ref.at[r], feats.at[:, pl.ds(r * U, U)], sem) for r in range(NR)]
    for copy in gets:
        copy.start()
    acc[...] = jnp.zeros_like(acc)

    def distances(n, out):
        own = col_ref[n, E:]
        out[...] = dot(jnp.concatenate([own, own, own], axis=0), feats[...], TN)

    def waves(n, dist):
        for i in range(0, U, 16):
            for j in range(0, NR * U, 512):
                d2 = dist[i : i + 16, j : j + 512]
                inv = lax.rsqrt(d2)
                turns = d2 * inv
                f = turns - jnp.round(turns)
                u = f * f
                s = f * (WAVE[0] + u * (WAVE[1] + u * (WAVE[2] + u * WAVE[3])))
                k_ref[n, i : i + 16, j : j + 512] = ((FACTOR - s * s) * inv).astype(BF)

    def accumulate(m):
        p = jnp.concatenate([col_ref[2 * m, :E], col_ref[2 * m + 1, :E]], axis=1)
        k = jnp.concatenate([k_ref[2 * m], k_ref[2 * m + 1]], axis=0)
        acc[...] += dot(p, k)

    def saved(n):
        return pltpu.make_async_copy(k_ref.at[pl.ds(2 * n, 2)], k_hbm.at[pl.ds(2 * n, 2)], sem)

    def pair(m):
        distances(2 * m + 1, dist_b)
        waves(2 * m, dist_a)
        distances(jnp.minimum(2 * m + 2, NC - 1), dist_a)
        waves(2 * m + 1, dist_b)
        saved(m).start()

    for copy in gets:
        copy.wait()
    distances(0, dist_a)
    pair(0)

    def step(m, carry):
        accumulate(m - 1)
        pair(m)
        return carry

    lax.fori_loop(1, NC // 2, step, 0)
    accumulate(NC // 2 - 1)
    write_partials(acc, out_ref)
    pltpu.make_async_copy(k_ref, k_hbm, sem).wait()


def make_kernel(cols, rows):
    return call(
        kernel_body,
        (hbm((NC, U, NR * U), BF), hbm((NR, 3, E, U), BF)),
        flops=40 * 2 * MB,
        moved=6 * MB,
        in_specs=[IN_VMEM, IN_HBM],
        out_specs=(IN_HBM, IN_VMEM),
        scratch_shapes=[
            pltpu.VMEM((E, NR * U), F32),
            pltpu.VMEM((48, NR * U), BF),
            pltpu.VMEM((U, NR * U), F32),
            pltpu.VMEM((U, NR * U), F32),
            pltpu.VMEM((NC, U, NR * U), BF),
            pltpu.SemaphoreType.DMA,
        ],
    )(cols, *keep(rows))


def product_body(p_ref, k_ref, out_ref, acc):
    acc[...] = jnp.zeros_like(acc)
    for n in range(0, NC, 4):
        p = jnp.concatenate([p_ref[n + i] for i in range(4)], axis=1)
        k = jnp.concatenate([k_ref[n + i] for i in range(4)], axis=0)
        acc[...] += dot(p, k)
    write_partials(acc, out_ref)


def product(present, kernel):
    return call(
        product_body,
        shape((NR, 3, E, U), BF),
        flops=2 * E * 2 * MB,
        moved=5 * MB,
        in_specs=[IN_VMEM, IN_VMEM],
        out_specs=IN_VMEM,
        scratch_shapes=[pltpu.VMEM((E, NR * U), F32)],
    )(present, kernel)


def span(b):
    return ((0, 2), (1, 3)) if b == 0 else ((6, 0), (7, 1)) if b == 2 else tuple((2 + i, i) for i in range(4))


def sweep_body(last, parity, own_ref, mid, near_a, near_b, far_a, far_b, inc, mid_metas, tiles_h, prev_h, nxt_h, edge_a_h, edge_b_h, *rest):
    if last:
        present_out, field_out = rest[:2]
    else:
        present_out, field_out = rest[0], None
    src, srcf, f1, fields, tiles, prev, nxt, edge_a, edge_b, moves_v, moves, sems = rest[2 if last else 1 :]
    loads = [(moves_v, moves), (tiles_h, tiles)]
    loads += [(h.at[pl.ds(0, 4 * ROWS)], v) for h, v in ((prev_h, prev), (nxt_h, nxt))]
    loads += [(edge_a_h, edge_a), (edge_b_h, edge_b)]
    odd = parity[0]
    partners = ((6 - 6 * odd, 2 * odd, 6 - 5 * odd, 3 * odd), (6 * odd, 2 - 2 * odd, 1 + 5 * odd, 3 - 3 * odd))
    loads = [pltpu.make_async_copy(a, b, sems.at[n]) for n, (a, b) in enumerate(loads)]
    for copy in loads[1:]:
        copy.start()

    def meta(br, bc):
        if bc == 1:
            return mid_metas[16 * br : 16 * br + 16].astype(F32)
        return (far_a, far_b)[bc // 2][TAIL + 16 * br : TAIL + 16 * br + 16].astype(F32)

    rows = []
    for b in range(9):
        o = meta(b // 3, b % 3)[2:3]
        rows.append(o + 5.0 * (jnp.where(o >= 3.0, 1.0, 0.0) + jnp.where(o >= 6.0, 1.0, 0.0)))
    lane = lax.broadcasted_iota(jnp.int32, (1, U), 1)
    for n in range(5):
        value = rows[2 * n] if n == 4 else jnp.where(lane < 64, rows[2 * n], pltpu.roll(rows[2 * n + 1], 64, 1))
        moves_v[n : n + 1] = value.astype(jnp.int32)
    loads[0].start()
    line = lax.broadcasted_iota(jnp.int32, (S, U), 0).astype(F32)

    def coupling(br, bc):
        m = meta(br, bc)
        return m[0:1], jnp.where(m[1:2] == line, 1.0, 0.0).astype(BF)

    def masked(c, hi, ids):
        ids = [t.astype(F32) if isinstance(t, jax.Array) else float(t) for t in ids]
        return jnp.concatenate([c * jnp.where(hi == t, 1.0, 0.0).astype(BF) for t in ids], axis=0)

    def place(br, bc):
        hi, lo = coupling(br, bc)
        c = (near_a, mid, near_b)[bc][br * E : br * E + E]
        C, j = (2, 0) if bc == 1 else partners[bc // 2][:2]
        places = [(R * 8 + C + n, i * 4 + j + n) for R, i in span(br) for n in range(4 if bc == 1 else 2)]
        out = dot(masked(c, hi, [t for _, t in places]), lo, NT).astype(BF)
        for n, (w, _) in enumerate(places):
            src[w] = out[n * E : n * E + E]

    hi, lo = coupling(1, 1)
    own = own_ref[...]
    top = own.astype(BF)
    low = (own - top.astype(F32)).astype(BF)
    both = jnp.concatenate([masked(top, hi, range(16)), masked(low, hi, range(16))], axis=1)
    twice = jnp.concatenate([lo, lo], axis=1)
    out = dot(both, twice, NT)
    for t in range(16):
        srcf[t] = out[t * E : t * E + E]
        src[(2 + t // 4) * 8 + 2 + t % 4] = out[t * E : t * E + E].astype(BF)
    for br in range(3):
        for bc in range(3):
            if br != 1 or bc != 1:
                place(br, bc)
    for copy in loads[:2]:
        copy.wait()

    def apply(values, base, block, tile, ref, start):
        total = None
        for h in range(2):
            ks = (2 * h, 2 * h + 1)
            x = jnp.concatenate([values[base + moves[block // 2, block % 2 * 64 + tile * 4 + k]] for k in ks], axis=1)
            a = [ref[start + k * S : start + k * S + S, :] for k in ks]
            y = dot(x, jnp.concatenate(a, axis=1), NT)
            total = y if total is None else total + y
        return total

    def own_tile(t, carry):
        i, j = t // 4, t % 4
        w = (2 + i) * 8 + 2 + j
        f1[w] = (srcf[t] + apply(src, w - 9, 4, t, tiles, t * ROWS)).astype(BF)
        return carry

    for t in range(16):
        own_tile(t, 0)
    for copy in loads[2:]:
        copy.wait()

    def halo(w, block, tile, ref, start):
        y = apply(src, w - 9, block, tile, ref, start)
        f1[w] = (src[w].astype(F32) + y).astype(BF)

    def edge_row(j, carry):
        halo(8 + 2 + j, 1, 12 + j, prev, j * 4 * S)
        halo(48 + 2 + j, 7, j, nxt, j * 4 * S)
        return carry

    for j in range(4):
        edge_row(j, 0)

    def edge_col(i, carry):
        w = (2 + i) * 8
        for n, ref in enumerate((edge_a, edge_b)):
            halo(w + partners[n][2], 3 + 2 * n, i * 4 + partners[n][3], ref, i * ROWS)
        return carry

    for i in range(4):
        edge_col(i, 0)
    for n, ref in enumerate((far_a, far_b)):
        halo(8 + partners[n][2], 2 * n, 12 + partners[n][3], ref, 0)
        halo(48 + partners[n][2], 6 + 2 * n, partners[n][3], ref, ROWS)

    def final_tile(t, carry):
        i, j = t // 4, t % 4
        w = (2 + i) * 8 + 2 + j
        field = srcf[t] + apply(f1, w - 9, 4, t, tiles, t * ROWS)
        if last:
            field_out[pl.ds(t, E, stride=16), :] = field
        a = field.astype(BF)
        fields[t, :, :S] = a
        fields[t, :, S:] = (field - a.astype(F32)).astype(BF)
        return carry

    for t in range(16):
        final_tile(t, 0)
    y = dot(fields[...].reshape(16 * E, 2 * S), jnp.concatenate([lo, lo], axis=0))
    read = jnp.zeros((E, U), F32)
    for t in range(16):
        read += jnp.where(hi == float(t), y[t * E : t * E + E], 0.0)
    present = (inc[...].astype(F32) + read).astype(BF)
    if last:
        present_out[...] = present
    else:
        for c in range(NC):
            present_out[c] = present


def sweep(last, *args):
    if last:
        out = (shape((E, U), BF), shape((E * 16, S), F32))
    else:
        out = shape((NC, E, U), BF)

    def body(*refs):
        sweep_body(last, *refs)

    return call(
        body,
        out,
        flops=2 * E * S * S * 4 * 52,
        moved=6 * MB,
        in_specs=[IN_SMEM] + [IN_VMEM] * 8 + [IN_HBM] * 5,
        out_specs=(IN_VMEM, IN_VMEM) if last else IN_VMEM,
        scratch_shapes=[
            pltpu.VMEM((64, E, S), BF),
            pltpu.VMEM((16, E, S), F32),
            pltpu.VMEM((64, E, S), BF),
            pltpu.VMEM((16, E, 2 * S), BF),
            pltpu.VMEM((16 * ROWS, S), BF),
            pltpu.VMEM((4 * ROWS, S), BF),
            pltpu.VMEM((4 * ROWS, S), BF),
            pltpu.VMEM((4 * ROWS, S), BF),
            pltpu.VMEM((4 * ROWS, S), BF),
            pltpu.VMEM((5, U), jnp.int32),
            pltpu.SMEM((5, U), jnp.int32),
            pltpu.SemaphoreType.DMA((6,)),
        ],
    )(*args[:9], *keep(*args[9:]))


def shift(axis):
    size = lax.axis_size(axis)
    up = [(i, i + 1) for i in range(size - 1)]
    return up, [(j, i) for i, j in up]


def per_device(traces, incident, points, coupling, volume_tiles, tile_columns):
    row_up, row_down = shift("row")
    parity = (lax.axis_index("col") % 2).reshape(1)
    swap_a = [(c, c ^ 1) for c in range(NC)]
    swap_b = [(c, ((c - 1) ^ 1) + 1) for c in range(1, NC - 1)]
    tiles = volume_tiles.reshape(16 * ROWS, S)
    rows, cols = pack(traces, points)
    rows = lax.all_to_all(rows, "row", 0, 0, tiled=True)
    cols = lax.all_to_all(cols, "col", 0, 0, tiled=True)
    edge_a, edge_b = fill(parity, tiles)
    edge_a = lax.ppermute(edge_a, "col", swap_a)
    edge_b = lax.ppermute(edge_b, "col", swap_b)
    up, down, meta = slices(coupling.reshape(1, U), tile_columns, tiles)
    prev = lax.ppermute(up, "row", row_up)
    nxt = lax.ppermute(down, "row", row_down)
    kernel, partials = make_kernel(cols, rows)
    got = lax.all_to_all(partials, "row", 0, 0, tiled=True)
    far_a, far_b, metas = corners(parity, prev, nxt, meta)
    far_a = lax.ppermute(far_a, "col", swap_a)
    far_b = lax.ppermute(far_b, "col", swap_b)
    for outer in range(2):
        last = outer == 1
        own, mid = near(got)
        near_b = lax.ppermute(mid, "col", swap_b)
        near_a = lax.ppermute(mid, "col", swap_a)
        out = sweep(
            last, parity, own, mid, near_a, near_b, far_a, far_b, incident, metas, tiles, prev, nxt, edge_a, edge_b
        )
        if not last:
            out = lax.all_to_all(out, "col", 0, 0, tiled=True)
            partials = product(out, kernel)
            got = lax.all_to_all(partials, "row", 0, 0, tiled=True)
    present, field = out
    return present, field.reshape(E, 4, 4, S)


def solution(mesh):
    in_specs = (
        P(None, ("row", "col")),
        P(None, ("row", "col")),
        P(None, ("row", "col")),
        P(("row", "col")),
        P("row", "col", None, None, None),
        P("row", "col", None),
    )
    out_specs = (P(None, ("row", "col")), P(None, "row", "col", None))
    return jax.shard_map(per_device, mesh=mesh, in_specs=in_specs, out_specs=out_specs, check_vma=False)
```
